512 devices in a mesh: head: 8 (over y_hi, x), blk: 64 (over y_lo, z, core).
Axes of the slice: x: 4, y: 8 (y_hi: 2, y_lo: 4; y = y_hi * 4 + y_lo), z: 8, core: 2. Of those that a mesh axis runs over, the one named last changes fastest.
Arguments:
- queries: bfloat16 [32768, 4096], P(('head', 'blk')), may hold values from -6 to 6
- keys: bfloat16 [32768, 1024], P(('head', 'blk')), may hold values from -6 to 6
- values: bfloat16 [32768, 1024], P(('head', 'blk')), may hold values from -6 to 6
- grad_out: bfloat16 [32768, 4096], P(('head', 'blk')), may hold values from -6 to 6
- order: int32 [512], replicated, may hold values from 0 to 511, each once
Outputs:
- grad_queries: bfloat16 [32768, 4096], P(('head', 'blk'))
- grad_keys: bfloat16 [32768, 1024], P(('head', 'blk'))
- grad_values: bfloat16 [32768, 1024], P(('head', 'blk'))
The draws below stay inside these ranges and needn't reach their ends.
Inputs may be any that keep to these rules, and one draw needn't show every extreme that they name: `order`: each value names one slot's pair of half-blocks, each exactly once.
All inputs are finite; a program needn't handle non-finite values.
Results may differ from the reference program's by a relative error of at most 0.024.
Values may be sent and summed in bfloat16 or wider, within the bound.
No kernel may reach another device: no remote copies, remote signals or barrier semaphores. Data moves between devices by JAX's collectives and lax.ppermute only.
A program may use at most 64 MiB of HBM per device.

```python
import jax
import jax.numpy as jnp
from jax import lax

TOK_DEV = 64
QH = 32
KVH = 8
HD = 128
REACH = 1
SLOTS = 512
TOKENS = 32768
N_HEAD = 8
N_BLK = 64


def draw_queries(key, part):
    base = jax.random.fold_in(key, 3)
    drawn = jnp.clip(jax.random.normal(base, (TOKENS, QH * HD), jnp.float32), -6.0, 6.0)
    return drawn.astype(jnp.bfloat16)


def draw_keys(key, part):
    base = jax.random.fold_in(key, 5)
    drawn = jnp.clip(jax.random.normal(base, (TOKENS, KVH * HD), jnp.float32), -6.0, 6.0)
    return drawn.astype(jnp.bfloat16)


def steps_of(stream_key, dims, shards, low, largest):
    factor_of, own = 1.0, jax.random.fold_in(stream_key, 6)
    for dim, parts in shards:
        heights = jnp.exp(jax.random.uniform(jax.random.fold_in(own, dim), (parts,), jnp.float32, low / len(shards), largest / len(shards)))
        factor_of = factor_of * jnp.repeat(heights, dims[dim] // parts).reshape([-1 if axis == dim else 1 for axis in range(len(dims))])
    return factor_of


def normal_values(stream_key, extent, scale, most, pieces=(), kind=jnp.bfloat16):
    gain = steps_of(stream_key, extent, pieces, -0.22, 0.18) if pieces else 1.0
    result = jax.random.normal(stream_key, extent, jnp.float32) * scale * gain
    return jnp.minimum(jnp.maximum(result, -most), most).astype(kind)


def setup_inputs(seed: int = 0) -> dict:
    key_list = jax.random.split(jax.random.key(seed), 6)
    queries = draw_queries(jax.random.fold_in(key_list[5], 71), 0)
    keys = draw_keys(jax.random.fold_in(key_list[5], 71), 0)
    values = normal_values(key_list[2], (TOKENS, KVH * HD), 1.0, 6.0, ((0, 512),))
    grad_out = normal_values(key_list[3], (TOKENS, QH * HD), 1.0, 6.0, ((0, 512),))
    order = jax.random.permutation(key_list[4], SLOTS).astype(jnp.int32)
    return dict(queries=queries, keys=keys, values=values, grad_out=grad_out, order=order)


def by_class(values_in, heads):
    shaped = values_in.reshape(N_HEAD, N_BLK, TOK_DEV, heads, HD).transpose(1, 0, 2, 3, 4)
    return shaped.reshape(N_BLK, N_HEAD * TOK_DEV, heads, HD)


def class_positions(order, block_class):
    local_rows = jnp.arange(N_HEAD * TOK_DEV, dtype=jnp.int32)
    slot_index = (local_rows // TOK_DEV) * N_BLK + block_class
    offset_in = local_rows % TOK_DEV
    half_rows = TOK_DEV // 2
    slot_place = order[slot_index]
    early_pos = slot_place * half_rows + offset_in
    late_pos = (2 * SLOTS - 1 - slot_place) * half_rows + offset_in - half_rows
    return jnp.where(offset_in < half_rows, early_pos, late_pos)


def to_storage(stacked, column_count):
    shaped = stacked.reshape(N_BLK, N_HEAD, TOK_DEV, column_count).transpose(1, 0, 2, 3)
    return shaped.reshape(N_HEAD * N_BLK * TOK_DEV, column_count)


def reference(queries, keys, values, grad_out, order):
    score_scale = HD ** -0.5
    row_count = N_HEAD * TOK_DEV
    group_size = QH // KVH
    query_all = by_class(queries, QH)
    key_all = by_class(keys, KVH)
    value_all = by_class(values, KVH)
    grad_all = by_class(grad_out, QH)
    late_rows = (jnp.arange(row_count, dtype=jnp.int32) % TOK_DEV) >= TOK_DEV // 2
    cycle_visible = late_rows[:, None] & jnp.logical_not(late_rows)[None, :]

    def per_class(running, block_class):
        key_acc, value_acc = running
        query_rows = query_all[block_class].astype(jnp.float32).reshape(row_count, KVH, group_size, HD)
        grad_rows = grad_all[block_class].astype(jnp.float32).reshape(row_count, KVH, group_size, HD)
        sources = [(block_class - offset) % N_BLK for offset in range(REACH + 1)]
        key_block = jnp.concatenate([key_all[source] for source in sources], axis=0).astype(jnp.float32)
        value_block = jnp.concatenate([value_all[source] for source in sources], axis=0).astype(jnp.float32)
        query_pos = class_positions(order, block_class)
        own_visible = query_pos[None, :] <= query_pos[:, None]
        visible = jnp.concatenate([own_visible] + [cycle_visible] * REACH, axis=1)
        logits = jnp.einsum("ikgd,jkd->kgij", query_rows, key_block) * score_scale
        row_top = jnp.max(jnp.where(visible, logits, -jnp.inf), axis=-1, keepdims=True)
        row_total = jnp.sum(jnp.where(visible, jnp.exp(logits - row_top), 0.0), axis=-1, keepdims=True)
        log_total = row_top + jnp.log(row_total)
        weights = jnp.where(visible, jnp.exp(logits - log_total), 0.0)
        weights_low = lax.optimization_barrier(weights.astype(jnp.bfloat16)).astype(jnp.float32)
        spread = jnp.einsum("ikgd,jkd->kgij", grad_rows, value_block)
        row_delta = jnp.sum(weights_low * spread, axis=-1, keepdims=True)
        slopes = lax.optimization_barrier((weights * (spread - row_delta)).astype(jnp.bfloat16)).astype(jnp.float32)
        query_grad = (jnp.einsum("kgij,jkd->ikgd", slopes, key_block) * score_scale).astype(jnp.bfloat16)
        key_grad = jnp.einsum("kgij,ikgd->jkd", slopes, query_rows) * score_scale
        value_grad = jnp.einsum("kgij,ikgd->jkd", weights_low, grad_rows)
        for offset in range(REACH + 1):
            source = sources[offset]
            key_acc = key_acc.at[source].add(key_grad[offset * row_count:(offset + 1) * row_count])
            value_acc = value_acc.at[source].add(value_grad[offset * row_count:(offset + 1) * row_count])
        return (key_acc, value_acc), query_grad.reshape(row_count, QH * HD)

    start = (jnp.zeros((N_BLK, row_count, KVH, HD), jnp.float32), jnp.zeros((N_BLK, row_count, KVH, HD), jnp.float32))
    finals, query_grads = lax.scan(per_class, start, jnp.arange(N_BLK, dtype=jnp.int32))
    key_acc, value_acc = finals
    grad_queries = to_storage(query_grads, QH * HD)
    grad_keys = to_storage(key_acc.reshape(N_BLK, row_count, KVH * HD), KVH * HD).astype(jnp.bfloat16)
    grad_values = to_storage(value_acc.reshape(N_BLK, row_count, KVH * HD), KVH * HD).astype(jnp.bfloat16)
    return (grad_queries, grad_keys, grad_values)
```

```python
import jax
import jax.numpy as jnp
from jax import lax
from jax.experimental import pallas as pl
from jax.experimental.pallas import tpu as pltpu
from jax.sharding import PartitionSpec as P

HD = 128
XN = 4
KV = 2
GROUP = 4
LOG2E = 1.4426950408889634
NEG = -1e30


def dot(left, right, left_dim, right_dim):
    return lax.dot_general(
        left, right, (((left_dim,), (right_dim,)), ((), ())), preferred_element_type=jnp.float32
    )


def attention_kernel(
    qpos_ref, kpos_ref, qg_ref, own_ref, far_ref, pown_ref, pfar_ref, dq_ref, dkv_ref, dprev_ref
):
    half = qg_ref.shape[1] // 2
    slots = qg_ref.shape[0]
    rows = slots * half
    scale = HD ** (-0.5)
    width = KV * GROUP * HD
    qpos = qpos_ref[...]
    kpos = kpos_ref[...]
    keys = kpos.shape[0]
    early_seen = kpos[:, 0:1] <= qpos[0:1, :]
    late_seen = kpos[:, 1:2] <= qpos[1:2, :]

    def columns(ref, start, stop, column):
        block = ref[:, start:stop, column : column + HD]
        return block.reshape(block.shape[0] * block.shape[1], HD)

    def tile(query, grad, key, value, seen, seen_from):
        logits = dot(key, query, 1, 1) * (scale * LOG2E)
        if seen_from == 0 and seen.shape[0] == key.shape[0]:
            logits = jnp.where(seen, logits, NEG)
        else:
            stop = seen_from + seen.shape[0]
            logits = jnp.concatenate(
                [
                    logits[:seen_from],
                    jnp.where(seen, logits[seen_from:stop], NEG),
                    logits[stop:],
                ],
                axis=0,
            )
        spread = dot(value, grad, 1, 1)
        top = jnp.max(logits, axis=0, keepdims=True)
        mass = jnp.exp2(logits - top)
        weights = mass * (1.0 / jnp.sum(mass, axis=0, keepdims=True))
        low = weights.astype(jnp.bfloat16)
        delta = jnp.sum(low.astype(jnp.float32) * spread, axis=0, keepdims=True)
        slopes = (weights * (spread - delta)).astype(jnp.bfloat16)
        return (
            dot(slopes, key, 0, 0) * scale,
            dot(slopes, query, 1, 0) * scale,
            dot(low, grad, 1, 0),
        )

    for kv in range(KV):
        parts = []
        for column in (kv * HD, (KV + kv) * HD):
            early = [columns(ref, 0, half, column) for ref in (own_ref, far_ref)]
            late = [columns(ref, half, 2 * half, column) for ref in (own_ref, far_ref)]
            before = [columns(ref, 0, half, column) for ref in (pown_ref, pfar_ref)]
            parts.append(jnp.concatenate(early + late + before, axis=0))
        key, value = parts
        key_sum = None
        value_sum = None
        for pair in range(GROUP // 2):
            heads = [kv * GROUP + pair * 2 + i for i in range(2)]
            for kind in range(2):
                start, stop = kind * half, (kind + 1) * half
                query = jnp.concatenate(
                    [columns(qg_ref, start, stop, h * HD) for h in heads], axis=0
                )
                grad = jnp.concatenate(
                    [columns(qg_ref, start, stop, width + h * HD) for h in heads], axis=0
                )
                if kind == 0:
                    dq, dk, dv = tile(query, grad, key[:keys], value[:keys], early_seen, 0)
                    early_key, early_value = dk, dv
                else:
                    dq, dk, dv = tile(query, grad, key, value, late_seen, keys)
                for i, h in enumerate(heads):
                    dq_ref[:, start:stop, h * HD : (h + 1) * HD] = (
                        dq[i * rows : (i + 1) * rows].reshape(slots, half, HD).astype(jnp.bfloat16)
                    )
            dk = jnp.concatenate([dk[:keys] + early_key, dk[keys:]], axis=0)
            dv = jnp.concatenate([dv[:keys] + early_value, dv[keys:]], axis=0)
            key_sum = dk if key_sum is None else key_sum + dk
            value_sum = dv if value_sum is None else value_sum + dv
        for total, column in ((key_sum, kv * HD), (value_sum, (KV + kv) * HD)):
            low = total.astype(jnp.bfloat16)
            for kind in range(2):
                dkv_ref[:, kind * half : (kind + 1) * half, column : column + HD] = low[
                    kind * keys : (kind + 1) * keys
                ].reshape(2 * slots, half, HD)
            dprev_ref[:, :, column : column + HD] = low[2 * keys :].reshape(2 * slots, half, HD)


def attention(qpos, kpos, qg, own, far, pown, pfar):
    slots, tok, _ = qg.shape
    lines = own.shape[2]
    return pl.pallas_call(
        attention_kernel,
        out_shape=(
            jax.ShapeDtypeStruct((slots, tok, KV * GROUP * HD), jnp.bfloat16),
            jax.ShapeDtypeStruct((2 * slots, tok, lines), jnp.bfloat16),
            jax.ShapeDtypeStruct((2 * slots, tok // 2, lines), jnp.bfloat16),
        ),
        compiler_params=pltpu.CompilerParams(vmem_limit_bytes=48 * 1024 * 1024),
    )(qpos, kpos, qg, own, far, pown, pfar)


def body(queries, keys, values, grad_out, order):
    groups = lax.axis_size("head")
    cycle = lax.axis_size("blk")
    mine = lax.axis_index("blk")
    tok = queries.shape[0]
    half = tok // 2
    slot_total = order.shape[0]
    teams = [list(range(t, t + XN)) for t in range(0, groups, XN)]
    ahead = [(i, (i + 1) % cycle) for i in range(cycle)]
    behind = [(j, i) for i, j in ahead]
    across = [(h, (h + XN) % groups) for h in range(groups)]
    across_ahead = [
        (h * cycle + b, ((h + XN) % groups) * cycle + (b + 1) % cycle)
        for h in range(groups)
        for b in range(cycle)
    ]

    def team_exchange(array):
        return lax.all_to_all(array, "head", 0, 0, tiled=True, axis_index_groups=teams)

    def packed(first, second):
        blocks = [a.reshape(tok, XN, a.shape[1] // XN) for a in (first, second)]
        return jnp.concatenate(blocks, axis=2).transpose(1, 0, 2)

    own = team_exchange(packed(keys, values))
    far = lax.ppermute(own, "head", across)
    pown = lax.ppermute(own[:, :half], "blk", ahead)
    pfar = lax.ppermute(own[:, :half], ("head", "blk"), across_ahead)
    qg = team_exchange(packed(queries, grad_out))

    team = lax.axis_index("head") // XN
    places = lax.dynamic_index_in_dim(order.reshape(groups, cycle), mine, axis=1, keepdims=False)
    places = jnp.where(team == 0, places, jnp.roll(places, -XN))
    offset = lax.iota(jnp.int32, half)
    early = (places[:, None] * half + offset[None, :]).reshape(groups * half)
    late = ((2 * slot_total - 1 - places)[:, None] * half + offset[None, :]).reshape(groups * half)
    kpos = jnp.stack([early, late], axis=1)
    qpos = jnp.stack([jnp.tile(p[: XN * half], 2) for p in (early, late)], axis=0)

    dq, dkv, dprev = attention(qpos, kpos, qg, own, far, pown, pfar)

    back = lax.ppermute(dprev, "blk", behind)
    dq = team_exchange(dq)
    front = (dkv[:, :half].astype(jnp.float32) + back.astype(jnp.float32)).astype(jnp.bfloat16)
    dkv = jnp.concatenate([front, dkv[:, half:]], axis=1)
    dkv = jnp.where(team == 0, dkv, jnp.roll(dkv, XN, axis=0))
    dkv = lax.all_to_all(dkv, "head", 0, 0, tiled=True)
    dkv = dkv[:XN].astype(jnp.float32) + dkv[XN:].astype(jnp.float32)
    dkv = dkv.astype(jnp.bfloat16).transpose(1, 0, 2)
    lines = KV * HD
    grad_queries = dq.transpose(1, 0, 2).reshape(queries.shape)
    grad_keys = dkv[:, :, :lines].reshape(keys.shape)
    grad_values = dkv[:, :, lines:].reshape(values.shape)
    return (grad_queries, grad_keys, grad_values)


def solution(mesh):
    rows = P(("head", "blk"), None)
    return jax.shard_map(
        body,
        mesh=mesh,
        in_specs=(rows, rows, rows, rows, P()),
        out_specs=(rows, rows, rows),
        check_vma=False,
    )
```

```python
import jax
import jax.numpy as jnp
from jax import lax
from jax.experimental import pallas as pl
from jax.experimental.pallas import tpu as pltpu
from jax.sharding import PartitionSpec as P

HD = 128
XN = 4
KV = 2
GROUP = 4
LOG2E = 1.4426950408889634
NEG = -1e30


def dot(left, right, left_dim, right_dim):
    return lax.dot_general(
        left, right, (((left_dim,), (right_dim,)), ((), ())), preferred_element_type=jnp.float32
    )


def attention_kernel(qpos_ref, kpos_ref, qg_ref, kv_ref, dq_ref, dkv_ref):
    half = qg_ref.shape[1] // 2
    slots = qg_ref.shape[0]
    rows = slots * half
    scale = HD ** (-0.5)
    width = KV * GROUP * HD
    qpos = qpos_ref[...]
    kpos = kpos_ref[...]
    keys = kpos.shape[0]
    places = [0, 2 * half, half, 3 * half, 4 * half, 5 * half]
    early_seen = kpos[:, 0:1] <= qpos[0:1, :]
    late_seen = kpos[:, 1:2] <= qpos[1:2, :]

    def columns(ref, start, stop, column):
        block = ref[:, start:stop, column : column + HD]
        return block.reshape(block.shape[0] * block.shape[1], HD)

    def tile(query, grad, key, value, seen, seen_from):
        logits = dot(key, query, 1, 1) * (scale * LOG2E)
        if seen_from == 0 and seen.shape[0] == key.shape[0]:
            logits = jnp.where(seen, logits, NEG)
        else:
            stop = seen_from + seen.shape[0]
            logits = jnp.concatenate(
                [
                    logits[:seen_from],
                    jnp.where(seen, logits[seen_from:stop], NEG),
                    logits[stop:],
                ],
                axis=0,
            )
        spread = dot(value, grad, 1, 1)
        top = jnp.max(logits, axis=0, keepdims=True)
        mass = jnp.exp2(logits - top)
        weights = mass * (1.0 / jnp.sum(mass, axis=0, keepdims=True))
        low = weights.astype(jnp.bfloat16)
        delta = jnp.sum(low.astype(jnp.float32) * spread, axis=0, keepdims=True)
        slopes = (weights * (spread - delta)).astype(jnp.bfloat16)
        return (
            dot(slopes, key, 0, 0) * scale,
            dot(slopes, query, 1, 0) * scale,
            dot(low, grad, 1, 0),
        )

    for kv in range(KV):
        parts = []
        for column in (kv * HD, (KV + kv) * HD):
            parts.append(
                jnp.concatenate([columns(kv_ref, r, r + half, column) for r in places], axis=0)
            )
        key, value = parts
        key_sum = None
        value_sum = None
        for pair in range(GROUP // 2):
            heads = [kv * GROUP + pair * 2 + i for i in range(2)]
            for kind in range(2):
                start, stop = kind * half, (kind + 1) * half
                query = jnp.concatenate(
                    [columns(qg_ref, start, stop, h * HD) for h in heads], axis=0
                )
                grad = jnp.concatenate(
                    [columns(qg_ref, start, stop, width + h * HD) for h in heads], axis=0
                )
                if kind == 0:
                    dq, dk, dv = tile(query, grad, key[:keys], value[:keys], early_seen, 0)
                    early_key, early_value = dk, dv
                else:
                    dq, dk, dv = tile(query, grad, key, value, late_seen, keys)
                for i, h in enumerate(heads):
                    dq_ref[:, start:stop, h * HD : (h + 1) * HD] = (
                        dq[i * rows : (i + 1) * rows].reshape(slots, half, HD).astype(jnp.bfloat16)
                    )
            dk = jnp.concatenate([dk[:keys] + early_key, dk[keys:]], axis=0)
            dv = jnp.concatenate([dv[:keys] + early_value, dv[keys:]], axis=0)
            key_sum = dk if key_sum is None else key_sum + dk
            value_sum = dv if value_sum is None else value_sum + dv
        for total, column in ((key_sum, kv * HD), (value_sum, (KV + kv) * HD)):
            low = total.astype(jnp.bfloat16)
            for i, r in enumerate(places):
                dkv_ref[:, r : r + half, column : column + HD] = low[
                    i * rows : (i + 1) * rows
                ].reshape(slots, half, HD)


def attention(qpos, kpos, qg, kv):
    slots, tok, _ = qg.shape
    return pl.pallas_call(
        attention_kernel,
        out_shape=(
            jax.ShapeDtypeStruct((slots, tok, KV * GROUP * HD), jnp.bfloat16),
            jax.ShapeDtypeStruct(kv.shape, jnp.bfloat16),
        ),
        compiler_params=pltpu.CompilerParams(vmem_limit_bytes=48 * 1024 * 1024),
    )(qpos, kpos, qg, kv)


def pack_kernel(query_ref, key_ref, value_ref, grad_ref, qg_ref, own_ref, early_ref):
    half = early_ref.shape[1]
    for x in range(XN):
        for refs, out in (((query_ref, grad_ref), qg_ref), ((key_ref, value_ref), own_ref)):
            wide = out.shape[2] // 2
            for i, ref in enumerate(refs):
                block = ref[:, x * wide : (x + 1) * wide]
                out[x, :, i * wide : (i + 1) * wide] = block
                if out is own_ref:
                    early_ref[x, :, i * wide : (i + 1) * wide] = block[:half]


def pack(queries, keys, values, grad_out):
    tok = queries.shape[0]
    wide = 2 * queries.shape[1] // XN
    lines = 2 * keys.shape[1] // XN
    return pl.pallas_call(
        pack_kernel,
        out_shape=(
            jax.ShapeDtypeStruct((XN, tok, wide), queries.dtype),
            jax.ShapeDtypeStruct((XN, tok, lines), keys.dtype),
            jax.ShapeDtypeStruct((XN, tok // 2, lines), keys.dtype),
        ),
        compiler_params=pltpu.CompilerParams(vmem_limit_bytes=16 * 1024 * 1024),
    )(queries, keys, values, grad_out)


def unpack_kernel(dq_ref, own_ref, far_ref, pown_ref, pfar_ref, query_ref, key_ref, value_ref):
    tok = far_ref.shape[1]
    half = tok // 2
    wide = dq_ref.shape[2]
    lines = KV * HD
    for x in range(XN):
        query_ref[:, x * wide : (x + 1) * wide] = dq_ref[x]
        for i, ref in enumerate((key_ref, value_ref)):
            source = slice(i * lines, (i + 1) * lines)
            target = slice(x * lines, (x + 1) * lines)
            total = own_ref[x, :tok, source].astype(jnp.float32)
            total = total + far_ref[x, :, source].astype(jnp.float32)
            before = pown_ref[x, :, source].astype(jnp.float32)
            before = before + pfar_ref[x, :, source].astype(jnp.float32)
            ref[:half, target] = (total[:half] + before).astype(ref.dtype)
            ref[half:, target] = total[half:].astype(ref.dtype)


def unpack(dq, own, far, pown, pfar):
    tok = dq.shape[1]
    shapes = [(tok, XN * dq.shape[2])] + [(tok, XN * KV * HD)] * 2
    return pl.pallas_call(
        unpack_kernel,
        out_shape=tuple(jax.ShapeDtypeStruct(shape, jnp.bfloat16) for shape in shapes),
        compiler_params=pltpu.CompilerParams(vmem_limit_bytes=16 * 1024 * 1024),
    )(dq, own, far, pown, pfar)


def body(queries, keys, values, grad_out, order):
    groups = lax.axis_size("head")
    cycle = lax.axis_size("blk")
    mine = lax.axis_index("blk")
    tok = queries.shape[0]
    half = tok // 2
    slot_total = order.shape[0]
    teams = [list(range(t, t + XN)) for t in range(0, groups, XN)]
    ahead = [(i, (i + 1) % cycle) for i in range(cycle)]
    behind = [(j, i) for i, j in ahead]
    across = [(h, (h + XN) % groups) for h in range(groups)]
    across_ahead = [
        (h * cycle + b, ((h + XN) % groups) * cycle + (b + 1) % cycle)
        for h in range(groups)
        for b in range(cycle)
    ]

    across_behind = [(j, i) for i, j in across_ahead]

    def team_exchange(array):
        return lax.all_to_all(array, "head", 0, 0, tiled=True, axis_index_groups=teams)

    qg, own, early_rows = pack(queries, keys, values, grad_out)
    far = lax.ppermute(own, "head", across)
    pown = lax.ppermute(early_rows, "blk", ahead)
    pfar = lax.ppermute(early_rows, ("head", "blk"), across_ahead)
    qg = team_exchange(qg)
    kv = team_exchange(jnp.concatenate([own, far, pown, pfar], axis=1))

    team = lax.axis_index("head") // XN
    places = lax.dynamic_index_in_dim(order.reshape(groups, cycle), mine, axis=1, keepdims=False)
    places = jnp.where(team == 0, places, jnp.roll(places, -XN))
    offset = lax.iota(jnp.int32, half)
    early = (places[:, None] * half + offset[None, :]).reshape(groups * half)
    late = ((2 * slot_total - 1 - places)[:, None] * half + offset[None, :]).reshape(groups * half)
    kpos = jnp.stack([early, late], axis=1)
    qpos = jnp.stack([jnp.tile(p[: XN * half], 2) for p in (early, late)], axis=0)

    dq, dkv = attention(qpos, kpos, qg, kv)

    dkv = team_exchange(dkv)
    dq, dkv = lax.optimization_barrier((dq, dkv))
    far = lax.ppermute(dkv[:, tok : 2 * tok], "head", across)
    pown = lax.ppermute(dkv[:, 2 * tok : 2 * tok + half], "blk", behind)
    pfar = lax.ppermute(dkv[:, 2 * tok + half :], ("head", "blk"), across_behind)
    dq = team_exchange(dq)
    return unpack(dq, dkv, far, pown, pfar)


def solution(mesh):
    rows = P(("head", "blk"), None)
    return jax.shard_map(
        body,
        mesh=mesh,
        in_specs=(rows, rows, rows, rows, P()),
        out_specs=(rows, rows, rows),
        check_vma=False,
    )
```

```python
import jax
import jax.numpy as jnp
from jax import lax
from jax.experimental import pallas as pl
from jax.experimental.pallas import tpu as pltpu
from jax.sharding import PartitionSpec as P

HD = 128
XN = 4
KV = 2
GROUP = 4
LOG2E = 1.4426950408889634
NEG = -1e30


def dot(left, right, left_dim, right_dim):
    return lax.dot_general(
        left, right, (((left_dim,), (right_dim,)), ((), ())), preferred_element_type=jnp.float32
    )


def attention_kernel(
    team_ref, qpos_ref, kpos_ref, qg_ref, own_ref, far_ref, pown_ref, pfar_ref, dq_ref, dkv_ref, dprev_ref
):
    half = qg_ref.shape[1] // 2
    slots = qg_ref.shape[0]
    rows = slots * half
    scale = HD ** (-0.5)
    width = KV * GROUP * HD
    qpos = qpos_ref[...]
    kpos = kpos_ref[...]
    keys = kpos.shape[0]
    early_seen = kpos[:, 0:1] <= qpos[0:1, :]
    late_seen = kpos[:, 1:2] <= qpos[1:2, :]

    def columns(ref, start, stop, column):
        block = ref[:, start:stop, column : column + HD]
        return block.reshape(block.shape[0] * block.shape[1], HD)

    def tile(query, grad, key, value, seen, seen_from):
        logits = dot(key, query, 1, 1) * (scale * LOG2E)
        if seen_from == 0 and seen.shape[0] == key.shape[0]:
            logits = jnp.where(seen, logits, NEG)
        else:
            stop = seen_from + seen.shape[0]
            logits = jnp.concatenate(
                [
                    logits[:seen_from],
                    jnp.where(seen, logits[seen_from:stop], NEG),
                    logits[stop:],
                ],
                axis=0,
            )
        spread = dot(value, grad, 1, 1)
        top = jnp.max(logits, axis=0, keepdims=True)
        mass = jnp.exp2(logits - top)
        weights = mass * (1.0 / jnp.sum(mass, axis=0, keepdims=True))
        low = weights.astype(jnp.bfloat16)
        delta = jnp.sum(low.astype(jnp.float32) * spread, axis=0, keepdims=True)
        slopes = (weights * (spread - delta)).astype(jnp.bfloat16)
        return (
            dot(slopes, key, 0, 0) * scale,
            dot(slopes, query, 1, 0) * scale,
            dot(low, grad, 1, 0),
        )

    for kv in range(KV):
        parts = []
        for column in (kv * HD, (KV + kv) * HD):
            early = [columns(ref, 0, half, column) for ref in (own_ref, far_ref)]
            late = [columns(ref, half, 2 * half, column) for ref in (own_ref, far_ref)]
            before = [columns(ref, 0, half, column) for ref in (pown_ref, pfar_ref)]
            parts.append(jnp.concatenate(early + late + before, axis=0))
        key, value = parts
        key_sum = None
        value_sum = None
        for pair in range(GROUP // 2):
            heads = [kv * GROUP + pair * 2 + i for i in range(2)]
            for kind in range(2):
                start, stop = kind * half, (kind + 1) * half
                query = jnp.concatenate(
                    [columns(qg_ref, start, stop, h * HD) for h in heads], axis=0
                )
                grad = jnp.concatenate(
                    [columns(qg_ref, start, stop, width + h * HD) for h in heads], axis=0
                )
                if kind == 0:
                    dq, dk, dv = tile(query, grad, key[:keys], value[:keys], early_seen, 0)
                    early_key, early_value = dk, dv
                else:
                    dq, dk, dv = tile(query, grad, key, value, late_seen, keys)
                for i, h in enumerate(heads):
                    dq_ref[:, start:stop, h * HD : (h + 1) * HD] = (
                        dq[i * rows : (i + 1) * rows].reshape(slots, half, HD).astype(jnp.bfloat16)
                    )
            dk = jnp.concatenate([dk[:keys] + early_key, dk[keys:]], axis=0)
            dv = jnp.concatenate([dv[:keys] + early_value, dv[keys:]], axis=0)
            key_sum = dk if key_sum is None else key_sum + dk
            value_sum = dv if value_sum is None else value_sum + dv
        for total, column in ((key_sum, kv * HD), (value_sum, (KV + kv) * HD)):
            low = total.astype(jnp.bfloat16)
            for side in range(2):
                first = pl.multiple_of(jnp.bitwise_xor(team_ref[0], side) * slots, slots)
                target = pl.ds(first, slots)
                for kind in range(3):
                    top = kind * keys + side * rows
                    block = low[top : top + rows].reshape(slots, half, HD)
                    if kind < 2:
                        dkv_ref[target, kind * half : (kind + 1) * half, column : column + HD] = block
                    else:
                        dprev_ref[target, :, column : column + HD] = block


def attention(team, qpos, kpos, qg, own, far, pown, pfar):
    slots, tok, _ = qg.shape
    lines = own.shape[2]
    return pl.pallas_call(
        attention_kernel,
        out_shape=(
            jax.ShapeDtypeStruct((slots, tok, KV * GROUP * HD), jnp.bfloat16),
            jax.ShapeDtypeStruct((2 * slots, tok, lines), jnp.bfloat16),
            jax.ShapeDtypeStruct((2 * slots, tok // 2, lines), jnp.bfloat16),
        ),
        in_specs=[pl.BlockSpec(memory_space=pltpu.SMEM)] + [pl.BlockSpec()] * 7,
        compiler_params=pltpu.CompilerParams(vmem_limit_bytes=48 * 1024 * 1024),
    )(team, qpos, kpos, qg, own, far, pown, pfar)


def pack_kernel(first_ref, second_ref, out_ref, sems):
    wide = out_ref.shape[2] // 2
    copies = []
    for x in range(XN):
        for i, ref in enumerate((first_ref, second_ref)):
            copies.append(
                pltpu.make_async_copy(
                    ref.at[:, x * wide : (x + 1) * wide],
                    out_ref.at[x, :, i * wide : (i + 1) * wide],
                    sems.at[2 * x + i],
                )
            )
    for copy in copies:
        copy.start()
    for copy in copies:
        copy.wait()


def pack(first, second):
    tok, columns = first.shape
    anywhere = pl.BlockSpec(memory_space=pl.ANY)
    return pl.pallas_call(
        pack_kernel,
        out_shape=jax.ShapeDtypeStruct((XN, tok, 2 * columns // XN), first.dtype),
        in_specs=[anywhere, anywhere],
        out_specs=anywhere,
        scratch_shapes=[pltpu.SemaphoreType.DMA((2 * XN,))],
    )(first, second)


def unpack_kernel(dq_ref, dkv_ref, query_ref, key_ref, value_ref):
    wide = dq_ref.shape[2]
    lines = KV * HD
    for x in range(XN):
        query_ref[:, x * wide : (x + 1) * wide] = dq_ref[x]
        for i, ref in enumerate((key_ref, value_ref)):
            source = slice(i * lines, (i + 1) * lines)
            total = dkv_ref[x, :, source].astype(jnp.float32)
            total = total + dkv_ref[XN + x, :, source].astype(jnp.float32)
            ref[:, x * lines : (x + 1) * lines] = total.astype(ref.dtype)


def unpack(dq, dkv):
    tok = dq.shape[1]
    shapes = [(tok, XN * dq.shape[2])] + [(tok, XN * KV * HD)] * 2
    return pl.pallas_call(
        unpack_kernel,
        out_shape=tuple(jax.ShapeDtypeStruct(shape, jnp.bfloat16) for shape in shapes),
        compiler_params=pltpu.CompilerParams(vmem_limit_bytes=16 * 1024 * 1024),
    )(dq, dkv)


def body(queries, keys, values, grad_out, order):
    groups = lax.axis_size("head")
    cycle = lax.axis_size("blk")
    mine = lax.axis_index("blk")
    tok = queries.shape[0]
    half = tok // 2
    slot_total = order.shape[0]
    teams = [list(range(t, t + XN)) for t in range(0, groups, XN)]
    ahead = [(i, (i + 1) % cycle) for i in range(cycle)]
    behind = [(j, i) for i, j in ahead]
    across = [(h, (h + XN) % groups) for h in range(groups)]
    def team_exchange(array):
        return lax.all_to_all(array, "head", 0, 0, tiled=True, axis_index_groups=teams)

    own = team_exchange(pack(keys, values))
    far = lax.ppermute(own, "head", across)
    pown = lax.ppermute(own[:, :half], "blk", ahead)
    qg = team_exchange(pack(queries, grad_out))
    pfar = lax.ppermute(far[:, :half], "blk", ahead)

    team = lax.axis_index("head") // XN
    places = lax.dynamic_index_in_dim(order.reshape(groups, cycle), mine, axis=1, keepdims=False)
    places = jnp.where(team == 0, places, jnp.roll(places, -XN))
    offset = lax.iota(jnp.int32, half)
    early = (places[:, None] * half + offset[None, :]).reshape(groups * half)
    late = ((2 * slot_total - 1 - places)[:, None] * half + offset[None, :]).reshape(groups * half)
    kpos = jnp.stack([early, late], axis=1)
    qpos = jnp.stack([jnp.tile(p[: XN * half], 2) for p in (early, late)], axis=0)

    sides = jnp.full((1,), team, jnp.int32)
    dq, dkv, dprev = attention(sides, qpos, kpos, qg, own, far, pown, pfar)

    back = lax.ppermute(dprev, "blk", behind)
    dq = team_exchange(dq)
    front = (dkv[:, :half].astype(jnp.float32) + back.astype(jnp.float32)).astype(jnp.bfloat16)
    dkv = jnp.concatenate([front, dkv[:, half:]], axis=1)
    dkv = lax.all_to_all(dkv, "head", 0, 0, tiled=True)
    return unpack(dq, dkv)


def solution(mesh):
    rows = P(("head", "blk"), None)
    return jax.shard_map(
        body,
        mesh=mesh,
        in_specs=(rows, rows, rows, rows, P()),
        out_specs=(rows, rows, rows),
        check_vma=False,
    )
```

```python
import jax
import jax.numpy as jnp
from jax import lax
from jax.experimental import pallas as pl
from jax.experimental.pallas import tpu as pltpu
from jax.sharding import PartitionSpec as P

HD = 128
GROUP = 4
QCOL = GROUP * HD
KEY, VALUE, GRAD, WIDE = QCOL, QCOL + HD, QCOL + 2 * HD, 2 * QCOL + 2 * HD
BACK = QCOL + 2 * HD
LOG2E = 1.4426950408889634
NEG = -1e30


def dot(left, right, left_dim, right_dim):
    return lax.dot_general(
        left, right, (((left_dim,), (right_dim,)), ((), ())), preferred_element_type=jnp.float32
    )


def params(mib):
    return pltpu.CompilerParams(vmem_limit_bytes=mib * 1024 * 1024)


def attention_kernel(qpos_ref, kpos_ref, data_ref, before_ref, out_ref, dbefore_ref):
    slots, tok, _ = data_ref.shape
    half = tok // 2
    rows = slots * half
    scale = HD ** (-0.5)
    qpos = qpos_ref[...]
    kpos = kpos_ref[...]
    early_seen = kpos[:, 0:1] <= qpos[0:1, :]
    late_seen = kpos[:, 1:2] <= qpos[1:2, :]

    def columns(ref, start, column):
        return ref[:, start : start + half, column : column + HD].reshape(rows, HD)

    def tile(query, grad, key, value, seen, seen_from):
        logits = dot(key, query, 1, 1) * (scale * LOG2E)
        if key.shape[0] == rows:
            logits = jnp.where(seen, logits, NEG)
        else:
            stop = seen_from + rows
            masked = jnp.where(seen, logits[seen_from:stop], NEG)
            logits = jnp.concatenate([logits[:seen_from], masked, logits[stop:]], axis=0)
        spread = dot(value, grad, 1, 1)
        top = jnp.max(logits, axis=0, keepdims=True)
        mass = jnp.exp2(logits - top)
        weights = mass * (1.0 / jnp.sum(mass, axis=0, keepdims=True))
        low = weights.astype(jnp.bfloat16)
        delta = jnp.sum(low.astype(jnp.float32) * spread, axis=0, keepdims=True)
        slopes = (weights * (spread - delta)).astype(jnp.bfloat16)
        return (
            dot(slopes, key, 0, 0) * scale,
            dot(slopes, query, 1, 0) * scale,
            dot(low, grad, 1, 0),
        )

    key, value = [
        jnp.concatenate(
            [
                columns(data_ref, 0, column),
                columns(data_ref, half, column),
                columns(before_ref, 0, column - KEY),
            ],
            axis=0,
        )
        for column in (KEY, VALUE)
    ]
    key_sum = None
    value_sum = None
    for head in range(GROUP):
        column = head * HD
        results = []
        for start in (0, half):
            query = columns(data_ref, start, column)
            grad = columns(data_ref, start, GRAD + column)
            if start == 0:
                result = tile(query, grad, key[:rows], value[:rows], early_seen, 0)
            else:
                result = tile(query, grad, key, value, late_seen, rows)
            out_ref[:, start : start + half, column : column + HD] = (
                result[0].reshape(slots, half, HD).astype(jnp.bfloat16)
            )
            results.append(result)
        (_, early_key, early_value), (_, dk, dv) = results
        dk = jnp.concatenate([dk[:rows] + early_key, dk[rows:]], axis=0)
        dv = jnp.concatenate([dv[:rows] + early_value, dv[rows:]], axis=0)
        key_sum = dk if key_sum is None else key_sum + dk
        value_sum = dv if value_sum is None else value_sum + dv
    for total, column in ((key_sum, KEY), (value_sum, VALUE)):
        low = total.astype(jnp.bfloat16)
        for i in range(2):
            out_ref[:, i * half : (i + 1) * half, column : column + HD] = low[
                i * rows : (i + 1) * rows
            ].reshape(slots, half, HD)
        dbefore_ref[:, :, column - KEY : column - KEY + HD] = low[2 * rows :].reshape(
            slots, half, HD
        )


def attention(qpos, kpos, data, before):
    slots, tok, _ = data.shape
    return pl.pallas_call(
        attention_kernel,
        out_shape=(
            jax.ShapeDtypeStruct((slots, tok, BACK), jnp.bfloat16),
            jax.ShapeDtypeStruct(before.shape, jnp.bfloat16),
        ),
        compiler_params=params(48),
    )(qpos, kpos, data, before)


def pack_kernel(query_ref, key_ref, value_ref, grad_ref, out_ref, q_buf, k_buf, v_buf, g_buf, sems):
    column = 0
    copies = []
    for i, (ref, buf) in enumerate(
        ((query_ref, q_buf), (key_ref, k_buf), (value_ref, v_buf), (grad_ref, g_buf))
    ):
        copies.append((pltpu.make_async_copy(ref, buf, sems.at[i]), buf))
        copies[i][0].start()
    groups = out_ref.shape[0]
    for copy, buf in copies:
        copy.wait()
        wide = buf.shape[1] // groups
        for h in range(groups):
            out_ref[h, :, column : column + wide] = buf[:, h * wide : (h + 1) * wide]
        column += wide


def pack(groups, *arrays):
    tok = arrays[0].shape[0]
    return pl.pallas_call(
        pack_kernel,
        out_shape=jax.ShapeDtypeStruct((groups, tok, WIDE), arrays[0].dtype),
        in_specs=[pl.BlockSpec(memory_space=pltpu.HBM)] * 4,
        scratch_shapes=[pltpu.VMEM(a.shape, a.dtype) for a in arrays]
        + [pltpu.SemaphoreType.DMA((4,))],
        compiler_params=params(16),
    )(*arrays)


def add_kernel(data_ref, back_ref, out_ref):
    half = back_ref.shape[1]
    out_ref[:, :, :KEY] = data_ref[:, :, :KEY]
    out_ref[:, half:, KEY:] = data_ref[:, half:, KEY:]
    total = data_ref[:, :half, KEY:].astype(jnp.float32) + back_ref[...].astype(jnp.float32)
    out_ref[:, :half, KEY:] = total.astype(out_ref.dtype)


def add_back(data, back):
    return pl.pallas_call(
        add_kernel,
        out_shape=jax.ShapeDtypeStruct(data.shape, data.dtype),
        compiler_params=params(16),
    )(data, back)


def unpack_kernel(data_ref, query_ref, key_ref, value_ref):
    for h in range(data_ref.shape[0]):
        query_ref[:, h * QCOL : (h + 1) * QCOL] = data_ref[h, :, :KEY]
        key_ref[:, h * HD : (h + 1) * HD] = data_ref[h, :, KEY:VALUE]
        value_ref[:, h * HD : (h + 1) * HD] = data_ref[h, :, VALUE:BACK]


def unpack(data):
    groups, tok, _ = data.shape
    widths = (groups * QCOL, groups * HD, groups * HD)
    return pl.pallas_call(
        unpack_kernel,
        out_shape=tuple(jax.ShapeDtypeStruct((tok, w), data.dtype) for w in widths),
        compiler_params=params(16),
    )(data)


def body(queries, keys, values, grad_out, order):
    groups = lax.axis_size("head")
    cycle = lax.axis_size("blk")
    mine = lax.axis_index("blk")
    half = queries.shape[0] // 2
    slot_total = order.shape[0]
    ahead = [(i, (i + 1) % cycle) for i in range(cycle)]
    behind = [(j, i) for i, j in ahead]

    def exchange(array):
        return lax.all_to_all(array, "head", 0, 0, tiled=True)

    data = exchange(pack(groups, queries, keys, values, grad_out))
    before = lax.ppermute(data[:, :half, KEY:GRAD], "blk", ahead)

    places = lax.dynamic_index_in_dim(order.reshape(groups, cycle), mine, axis=1, keepdims=False)
    offset = lax.iota(jnp.int32, half)
    early = (places[:, None] * half + offset[None, :]).reshape(groups * half)
    late = ((2 * slot_total - 1 - places)[:, None] * half + offset[None, :]).reshape(groups * half)
    kpos = jnp.stack([early, late], axis=1)
    qpos = jnp.stack([early, late], axis=0)

    out, dbefore = attention(qpos, kpos, data, before)
    back = lax.ppermute(dbefore, "blk", behind)
    return unpack(exchange(add_back(out, back)))


def solution(mesh):
    rows = P(("head", "blk"), None)
    return jax.shard_map(
        body,
        mesh=mesh,
        in_specs=(rows, rows, rows, rows, P()),
        out_specs=(rows, rows, rows),
        check_vma=False,
    )
```

```python
import jax
import jax.numpy as jnp
from jax import lax
from jax.experimental import pallas as pl
from jax.experimental.pallas import tpu as pltpu
from jax.sharding import PartitionSpec as P

HD = 128
XN = 4
KV = 2
GROUP = 4
QCOL = KV * GROUP * HD
KEY, VALUE, GRAD, WIDE = QCOL, QCOL + KV * HD, QCOL + 2 * KV * HD, 2 * QCOL + 2 * KV * HD
LINES = 2 * KV * HD
LOG2E = 1.4426950408889634
NEG = -1e30


def dot(left, right, left_dim, right_dim):
    return lax.dot_general(
        left, right, (((left_dim,), (right_dim,)), ((), ())), preferred_element_type=jnp.float32
    )


def params(mib):
    return pltpu.CompilerParams(vmem_limit_bytes=mib * 1024 * 1024)


def columns(ref, start, stop, column):
    block = ref[:, start:stop, column : column + HD]
    return block.reshape(block.shape[0] * block.shape[1], HD)


def tile(query, grad, key, value, seen, seen_from):
    scale = HD ** (-0.5)
    logits = dot(key, query, 1, 1) * (scale * LOG2E)
    stop = seen_from + seen.shape[0]
    masked = jnp.where(seen, logits[seen_from:stop], NEG)
    if seen.shape[0] == key.shape[0]:
        logits = masked
    else:
        logits = jnp.concatenate([logits[:seen_from], masked, logits[stop:]], axis=0)
    spread = dot(value, grad, 1, 1)
    top = jnp.max(logits, axis=0, keepdims=True)
    mass = jnp.exp2(logits - top)
    weights = mass * (1.0 / jnp.sum(mass, axis=0, keepdims=True))
    low = weights.astype(jnp.bfloat16)
    delta = jnp.sum(low.astype(jnp.float32) * spread, axis=0, keepdims=True)
    slopes = (weights * (spread - delta)).astype(jnp.bfloat16)
    return (
        dot(slopes, key, 0, 0) * scale,
        dot(slopes, query, 1, 0) * scale,
        dot(low, grad, 1, 0),
    )


def attend(data_ref, dq_ref, kv, start, stop, out_start, key, value, seen, seen_from):
    slots = data_ref.shape[0]
    rows = slots * (stop - start)
    key_sum = None
    value_sum = None
    for pair in range(GROUP // 2):
        heads = [kv * GROUP + pair * 2 + i for i in range(2)]
        query, grad = [
            jnp.concatenate(
                [columns(data_ref, start, stop, first + h * HD) for h in heads], axis=0
            )
            for first in (0, GRAD)
        ]
        dq, dk, dv = tile(query, grad, key, value, seen, seen_from)
        for i, h in enumerate(heads):
            dq_ref[:, out_start : out_start + stop - start, h * HD : (h + 1) * HD] = (
                dq[i * rows : (i + 1) * rows]
                .reshape(slots, stop - start, HD)
                .astype(jnp.bfloat16)
            )
        key_sum = dk if key_sum is None else key_sum + dk
        value_sum = dv if value_sum is None else value_sum + dv
    return key_sum, value_sum


def early_kernel(qpos_ref, kpos_ref, data_ref, far_ref, dq_ref, dkv_ref):
    half = data_ref.shape[1] // 2
    seen = kpos_ref[:, 0:1] <= qpos_ref[0:1, :]
    for kv in range(KV):
        key, value = [
            jnp.concatenate(
                [
                    columns(data_ref, 0, half, KEY + column),
                    columns(far_ref, 0, half, column),
                ],
                axis=0,
            )
            for column in (kv * HD, (KV + kv) * HD)
        ]
        sums = attend(data_ref, dq_ref, kv, 0, half, 0, key, value, seen, 0)
        for i, total in enumerate(sums):
            dkv_ref[2 * kv + i] = total


def late_kernel(
    team_ref,
    qpos_ref,
    kpos_ref,
    data_ref,
    far_ref,
    pown_ref,
    pfar_ref,
    dqe_ref,
    dkve_ref,
    dq_ref,
    dkv_ref,
    dprev_ref,
):
    slots, tok, _ = data_ref.shape
    half = tok // 2
    rows = slots * half
    keys = kpos_ref.shape[0]
    seen = kpos_ref[:, 1:2] <= qpos_ref[1:2, :]
    dq_ref[:, :half, :] = dqe_ref[...]
    for kv in range(KV):
        key, value = [
            jnp.concatenate(
                [
                    columns(data_ref, 0, half, KEY + column),
                    columns(far_ref, 0, half, column),
                    columns(data_ref, half, tok, KEY + column),
                    columns(far_ref, half, tok, column),
                    columns(pown_ref, 0, half, column),
                    columns(pfar_ref, 0, half, column),
                ],
                axis=0,
            )
            for column in (kv * HD, (KV + kv) * HD)
        ]
        sums = attend(data_ref, dq_ref, kv, half, tok, half, key, value, seen, keys)
        for i, total in enumerate(sums):
            column = (i * KV + kv) * HD
            first = (total[:keys] + dkve_ref[2 * kv + i]).astype(jnp.bfloat16)
            low = jnp.concatenate([first, total[keys:].astype(jnp.bfloat16)], axis=0)
            for side in range(2):
                at = pl.multiple_of(jnp.bitwise_xor(team_ref[0], side) * slots, slots)
                target = pl.ds(at, slots)
                for kind in range(3):
                    top = kind * keys + side * rows
                    block = low[top : top + rows].reshape(slots, half, HD)
                    if kind < 2:
                        dkv_ref[target, kind * half : (kind + 1) * half, column : column + HD] = block
                    else:
                        dprev_ref[target, :, column : column + HD] = block


def early_part(qpos, kpos, data, far):
    slots, tok, _ = data.shape
    return pl.pallas_call(
        early_kernel,
        out_shape=(
            jax.ShapeDtypeStruct((slots, tok // 2, QCOL), jnp.bfloat16),
            jax.ShapeDtypeStruct((2 * KV, kpos.shape[0], HD), jnp.float32),
        ),
        compiler_params=params(40),
    )(qpos, kpos, data, far)


def late_part(team, *arrays):
    slots, tok, _ = arrays[2].shape
    return pl.pallas_call(
        late_kernel,
        out_shape=(
            jax.ShapeDtypeStruct((slots, tok, QCOL), jnp.bfloat16),
            jax.ShapeDtypeStruct((2 * slots, tok, LINES), jnp.bfloat16),
            jax.ShapeDtypeStruct((2 * slots, tok // 2, LINES), jnp.bfloat16),
        ),
        in_specs=[pl.BlockSpec(memory_space=pltpu.SMEM)] + [pl.BlockSpec()] * len(arrays),
        compiler_params=params(48),
    )(team, *arrays)


def pack_kernel(query_ref, key_ref, value_ref, grad_ref, out_ref, q_buf, k_buf, v_buf, g_buf, sems):
    column = 0
    copies = []
    for i, (ref, buf) in enumerate(
        ((query_ref, q_buf), (key_ref, k_buf), (value_ref, v_buf), (grad_ref, g_buf))
    ):
        copies.append((pltpu.make_async_copy(ref, buf, sems.at[i]), buf))
        copies[i][0].start()
    groups = out_ref.shape[0]
    for copy, buf in copies:
        copy.wait()
        wide = buf.shape[1] // groups
        for h in range(groups):
            out_ref[h, :, column : column + wide] = buf[:, h * wide : (h + 1) * wide]
        column += wide


def pack(groups, *arrays):
    tok = arrays[0].shape[0]
    return pl.pallas_call(
        pack_kernel,
        out_shape=jax.ShapeDtypeStruct((groups, tok, WIDE), arrays[0].dtype),
        in_specs=[pl.BlockSpec(memory_space=pltpu.HBM)] * 4,
        scratch_shapes=[pltpu.VMEM(a.shape, a.dtype) for a in arrays]
        + [pltpu.SemaphoreType.DMA((4,))],
    )(*arrays)


def unpack_kernel(dq_ref, dkv_ref, query_ref, key_ref, value_ref):
    wide = dq_ref.shape[2]
    lines = KV * HD
    for x in range(XN):
        query_ref[:, x * wide : (x + 1) * wide] = dq_ref[x]
        for i, ref in enumerate((key_ref, value_ref)):
            source = slice(i * lines, (i + 1) * lines)
            total = dkv_ref[x, :, source].astype(jnp.float32)
            total = total + dkv_ref[XN + x, :, source].astype(jnp.float32)
            ref[:, x * lines : (x + 1) * lines] = total.astype(ref.dtype)


def unpack(dq, dkv):
    tok = dq.shape[1]
    shapes = [(tok, XN * dq.shape[2])] + [(tok, XN * KV * HD)] * 2
    return pl.pallas_call(
        unpack_kernel,
        out_shape=tuple(jax.ShapeDtypeStruct(shape, jnp.bfloat16) for shape in shapes),
        compiler_params=params(16),
    )(dq, dkv)


def body(queries, keys, values, grad_out, order):
    groups = lax.axis_size("head")
    cycle = lax.axis_size("blk")
    mine = lax.axis_index("blk")
    tok = queries.shape[0]
    half = tok // 2
    slot_total = order.shape[0]
    teams = [list(range(t, t + XN)) for t in range(0, groups, XN)]
    ahead = [(i, (i + 1) % cycle) for i in range(cycle)]
    behind = [(j, i) for i, j in ahead]
    across = [(h, (h + XN) % groups) for h in range(groups)]
    def team_exchange(array):
        return lax.all_to_all(array, "head", 0, 0, tiled=True, axis_index_groups=teams)

    data = team_exchange(pack(XN, queries, keys, values, grad_out))
    far = lax.ppermute(data[:, :, KEY:GRAD], "head", across)
    pown = lax.ppermute(data[:, :half, KEY:GRAD], "blk", ahead)
    pfar = lax.ppermute(far[:, :half], "blk", ahead)

    team = lax.axis_index("head") // XN
    places = lax.dynamic_index_in_dim(order.reshape(groups, cycle), mine, axis=1, keepdims=False)
    places = jnp.where(team == 0, places, jnp.roll(places, -XN))
    offset = lax.iota(jnp.int32, half)
    early = (places[:, None] * half + offset[None, :]).reshape(groups * half)
    late = ((2 * slot_total - 1 - places)[:, None] * half + offset[None, :]).reshape(groups * half)
    kpos = jnp.stack([early, late], axis=1)
    qpos = jnp.stack([jnp.tile(p[: XN * half], 2) for p in (early, late)], axis=0)

    sides = jnp.full((1,), team, jnp.int32)
    dq_early, dkv_early = early_part(qpos, kpos, data, far)
    dq, dkv, dprev = late_part(
        sides, qpos, kpos, data, far, pown, pfar, dq_early, dkv_early
    )

    back = lax.ppermute(dprev, "blk", behind)
    dq = team_exchange(dq)
    front = (dkv[:, :half].astype(jnp.float32) + back.astype(jnp.float32)).astype(jnp.bfloat16)
    dkv = jnp.concatenate([front, dkv[:, half:]], axis=1)
    dkv = lax.all_to_all(dkv, "head", 0, 0, tiled=True)
    return unpack(dq, dkv)


def solution(mesh):
    rows = P(("head", "blk"), None)
    return jax.shard_map(
        body,
        mesh=mesh,
        in_specs=(rows, rows, rows, rows, P()),
        out_specs=(rows, rows, rows),
        check_vma=False,
    )
```

```python
import jax
import jax.numpy as jnp
from jax import lax
from jax.experimental import pallas as pl
from jax.experimental.pallas import tpu as pltpu
from jax.sharding import PartitionSpec as P

HD = 128
XN = 4
KV = 2
GROUP = 4
LOG2E = 1.4426950408889634
NEG = -1e30


def dot(left, right, left_dim, right_dim):
    return lax.dot_general(
        left, right, (((left_dim,), (right_dim,)), ((), ())), preferred_element_type=jnp.float32
    )


def attention_kernel(qpos_ref, kpos_ref, qg_ref, kv_ref, prev_ref, dq_ref, dkv_ref, dprev_ref):
    half = qg_ref.shape[1] // 2
    slots = qg_ref.shape[0]
    rows = slots * half
    scale = HD ** (-0.5)
    width = KV * GROUP * HD
    qpos = qpos_ref[...]
    kpos = kpos_ref[...]
    keys = kpos.shape[0]
    early_seen = kpos[:, 0:1] <= qpos[0:1, :]
    late_seen = kpos[:, 1:2] <= qpos[1:2, :]

    def columns(ref, start, stop, column):
        block = ref[:, start:stop, column : column + HD]
        return block.reshape(block.shape[0] * block.shape[1], HD)

    def tile(query, grad, key, value, seen, seen_from):
        logits = dot(key, query, 1, 1) * (scale * LOG2E)
        if seen_from == 0 and seen.shape[0] == key.shape[0]:
            logits = jnp.where(seen, logits, NEG)
        else:
            stop = seen_from + seen.shape[0]
            logits = jnp.concatenate(
                [
                    logits[:seen_from],
                    jnp.where(seen, logits[seen_from:stop], NEG),
                    logits[stop:],
                ],
                axis=0,
            )
        spread = dot(value, grad, 1, 1)
        top = jnp.max(logits, axis=0, keepdims=True)
        mass = jnp.exp2(logits - top)
        weights = mass * (1.0 / jnp.sum(mass, axis=0, keepdims=True))
        low = weights.astype(jnp.bfloat16)
        delta = jnp.sum(low.astype(jnp.float32) * spread, axis=0, keepdims=True)
        slopes = (weights * (spread - delta)).astype(jnp.bfloat16)
        return (
            dot(slopes, key, 0, 0) * scale,
            dot(slopes, query, 1, 0) * scale,
            dot(low, grad, 1, 0),
        )

    for kv in range(KV):
        parts = []
        for column in (kv * HD, (KV + kv) * HD):
            parts.append(
                jnp.concatenate(
                    [
                        columns(kv_ref, 0, half, column),
                        columns(kv_ref, half, 2 * half, column),
                        columns(prev_ref, 0, half, column),
                    ],
                    axis=0,
                )
            )
        key, value = parts
        key_sum = None
        value_sum = None
        for pair in range(GROUP // 2):
            heads = [kv * GROUP + pair * 2 + i for i in range(2)]
            for kind in range(2):
                start, stop = kind * half, (kind + 1) * half
                query = jnp.concatenate(
                    [columns(qg_ref, start, stop, h * HD) for h in heads], axis=0
                )
                grad = jnp.concatenate(
                    [columns(qg_ref, start, stop, width + h * HD) for h in heads], axis=0
                )
                if kind == 0:
                    dq, dk, dv = tile(query, grad, key[:keys], value[:keys], early_seen, 0)
                    early_key, early_value = dk, dv
                else:
                    dq, dk, dv = tile(query, grad, key, value, late_seen, keys)
                for i, h in enumerate(heads):
                    dq_ref[:, start:stop, h * HD : (h + 1) * HD] = (
                        dq[i * rows : (i + 1) * rows].reshape(slots, half, HD).astype(jnp.bfloat16)
                    )
            dk = jnp.concatenate([dk[:keys] + early_key, dk[keys:]], axis=0)
            dv = jnp.concatenate([dv[:keys] + early_value, dv[keys:]], axis=0)
            key_sum = dk if key_sum is None else key_sum + dk
            value_sum = dv if value_sum is None else value_sum + dv
        for total, column in ((key_sum, kv * HD), (value_sum, (KV + kv) * HD)):
            low = total.astype(jnp.bfloat16)
            for kind in range(3):
                block = low[kind * keys : (kind + 1) * keys].reshape(2 * slots, half, HD)
                if kind < 2:
                    dkv_ref[:, kind * half : (kind + 1) * half, column : column + HD] = block
                else:
                    dprev_ref[:, :, column : column + HD] = block


def attention(qpos, kpos, qg, kv, prev):
    slots, tok, _ = qg.shape
    return pl.pallas_call(
        attention_kernel,
        out_shape=(
            jax.ShapeDtypeStruct((slots, tok, KV * GROUP * HD), jnp.bfloat16),
            jax.ShapeDtypeStruct(kv.shape, jnp.bfloat16),
            jax.ShapeDtypeStruct(prev.shape, jnp.bfloat16),
        ),
        compiler_params=pltpu.CompilerParams(vmem_limit_bytes=48 * 1024 * 1024),
    )(qpos, kpos, qg, kv, prev)


def pack_kernel(first_ref, second_ref, out_ref, first_buf, second_buf, sems):
    pairs = ((first_ref, first_buf), (second_ref, second_buf))
    copies = [pltpu.make_async_copy(ref, buf, sems.at[i]) for i, (ref, buf) in enumerate(pairs)]
    for copy in copies:
        copy.start()
    wide = out_ref.shape[2] // 2
    for i, (_, buf) in enumerate(pairs):
        copies[i].wait()
        for block in range(out_ref.shape[0]):
            x = block % XN
            out_ref[block, :, i * wide : (i + 1) * wide] = buf[:, x * wide : (x + 1) * wide]


def pack(blocks, first, second):
    tok, total = first.shape
    return pl.pallas_call(
        pack_kernel,
        out_shape=jax.ShapeDtypeStruct((blocks, tok, 2 * total // XN), first.dtype),
        in_specs=[pl.BlockSpec(memory_space=pl.ANY)] * 2,
        scratch_shapes=[
            pltpu.VMEM(first.shape, first.dtype),
            pltpu.VMEM(second.shape, second.dtype),
            pltpu.SemaphoreType.DMA((2,)),
        ],
    )(first, second)


def unpack_kernel(dq_ref, dkv_ref, query_ref, key_ref, value_ref):
    wide = dq_ref.shape[2]
    lines = KV * HD
    for x in range(XN):
        query_ref[:, x * wide : (x + 1) * wide] = dq_ref[x]
        for i, ref in enumerate((key_ref, value_ref)):
            source = slice(i * lines, (i + 1) * lines)
            total = dkv_ref[x, :, source].astype(jnp.float32)
            total = total + dkv_ref[XN + x, :, source].astype(jnp.float32)
            ref[:, x * lines : (x + 1) * lines] = total.astype(ref.dtype)


def unpack(dq, dkv):
    tok = dq.shape[1]
    shapes = [(tok, XN * dq.shape[2])] + [(tok, XN * KV * HD)] * 2
    return pl.pallas_call(
        unpack_kernel,
        out_shape=tuple(jax.ShapeDtypeStruct(shape, jnp.bfloat16) for shape in shapes),
        compiler_params=pltpu.CompilerParams(vmem_limit_bytes=16 * 1024 * 1024),
    )(dq, dkv)


def body(queries, keys, values, grad_out, order):
    groups = lax.axis_size("head")
    cycle = lax.axis_size("blk")
    mine = lax.axis_index("blk")
    tok = queries.shape[0]
    half = tok // 2
    slot_total = order.shape[0]
    teams = [list(range(t, t + XN)) for t in range(0, groups, XN)]
    ahead = [(i, (i + 1) % cycle) for i in range(cycle)]
    behind = [(j, i) for i, j in ahead]

    def team_exchange(array):
        return lax.all_to_all(array, "head", 0, 0, tiled=True, axis_index_groups=teams)

    def exchange(array):
        return lax.all_to_all(array, "head", 0, 0, tiled=True)

    kv = exchange(pack(groups, keys, values))
    prev = lax.ppermute(kv[:, :half], "blk", ahead)
    qg = pack(XN, queries, grad_out)
    qg, kv = lax.optimization_barrier((qg, kv))
    qg = team_exchange(qg)

    places = lax.dynamic_index_in_dim(order.reshape(groups, cycle), mine, axis=1, keepdims=False)
    offset = lax.iota(jnp.int32, half)
    early = (places[:, None] * half + offset[None, :]).reshape(groups * half)
    late = ((2 * slot_total - 1 - places)[:, None] * half + offset[None, :]).reshape(groups * half)
    kpos = jnp.stack([early, late], axis=1)
    team = lax.axis_index("head") // XN
    here = [lax.dynamic_slice_in_dim(p, team * XN * half, XN * half) for p in (early, late)]
    qpos = jnp.stack([jnp.tile(p, 2) for p in here], axis=0)

    dq, dkv, dprev = attention(qpos, kpos, qg, kv, prev)

    back = lax.ppermute(dprev, "blk", behind)
    dq = team_exchange(dq)
    front = (dkv[:, :half].astype(jnp.float32) + back.astype(jnp.float32)).astype(jnp.bfloat16)
    dkv = jnp.concatenate([front, dkv[:, half:]], axis=1)
    return unpack(dq, exchange(dkv))


def solution(mesh):
    rows = P(("head", "blk"), None)
    return jax.shard_map(
        body,
        mesh=mesh,
        in_specs=(rows, rows, rows, rows, P()),
        out_specs=(rows, rows, rows),
        check_vma=False,
    )
```

```python
import jax
import jax.numpy as jnp
from jax import lax
from jax.experimental import pallas as pl
from jax.experimental.pallas import tpu as pltpu
from jax.sharding import PartitionSpec as P

HD = 128
XN = 4
KV = 2
GROUP = 4
LOG2E = 1.4426950408889634
NEG = -1e30


def dot(left, right, left_dim, right_dim):
    return lax.dot_general(
        left, right, (((left_dim,), (right_dim,)), ((), ())), preferred_element_type=jnp.float32
    )


def attention_kernel(qpos_ref, kpos_ref, qg_ref, kv_ref, prev_ref, dq_ref, dkv_ref, dprev_ref):
    half = qg_ref.shape[1] // 2
    slots = qg_ref.shape[0]
    rows = slots * half
    scale = HD ** (-0.5)
    width = KV * GROUP * HD
    qpos = qpos_ref[...]
    kpos = kpos_ref[...]
    keys = kpos.shape[0]
    early_seen = kpos[:, 0:1] <= qpos[0:1, :]
    late_seen = kpos[:, 1:2] <= qpos[1:2, :]

    def columns(ref, start, stop, column):
        block = ref[:, start:stop, column : column + HD]
        return block.reshape(block.shape[0] * block.shape[1], HD)

    def tile(query, grad, key, value, seen, seen_from):
        logits = dot(key, query, 1, 1) * (scale * LOG2E)
        if seen_from == 0 and seen.shape[0] == key.shape[0]:
            logits = jnp.where(seen, logits, NEG)
        else:
            stop = seen_from + seen.shape[0]
            logits = jnp.concatenate(
                [
                    logits[:seen_from],
                    jnp.where(seen, logits[seen_from:stop], NEG),
                    logits[stop:],
                ],
                axis=0,
            )
        spread = dot(value, grad, 1, 1)
        top = jnp.max(logits, axis=0, keepdims=True)
        mass = jnp.exp2(logits - top)
        weights = mass * (1.0 / jnp.sum(mass, axis=0, keepdims=True))
        low = weights.astype(jnp.bfloat16)
        delta = jnp.sum(low.astype(jnp.float32) * spread, axis=0, keepdims=True)
        slopes = (weights * (spread - delta)).astype(jnp.bfloat16)
        return (
            dot(slopes, key, 0, 0) * scale,
            dot(slopes, query, 1, 0) * scale,
            dot(low, grad, 1, 0),
        )

    for kv in range(KV):
        parts = []
        for column in (kv * HD, (KV + kv) * HD):
            parts.append(
                jnp.concatenate(
                    [
                        columns(kv_ref, 0, half, column),
                        columns(kv_ref, half, 2 * half, column),
                        columns(prev_ref, 0, half, column),
                    ],
                    axis=0,
                )
            )
        key, value = parts
        key_sum = None
        value_sum = None
        for pair in range(GROUP // 2):
            heads = [kv * GROUP + pair * 2 + i for i in range(2)]
            for kind in range(2):
                start, stop = kind * half, (kind + 1) * half
                query = jnp.concatenate(
                    [columns(qg_ref, start, stop, h * HD) for h in heads], axis=0
                )
                grad = jnp.concatenate(
                    [columns(qg_ref, start, stop, width + h * HD) for h in heads], axis=0
                )
                if kind == 0:
                    dq, dk, dv = tile(query, grad, key[:keys], value[:keys], early_seen, 0)
                    early_key, early_value = dk, dv
                else:
                    dq, dk, dv = tile(query, grad, key, value, late_seen, keys)
                for i, h in enumerate(heads):
                    dq_ref[:, start:stop, h * HD : (h + 1) * HD] = (
                        dq[i * rows : (i + 1) * rows].reshape(slots, half, HD).astype(jnp.bfloat16)
                    )
            dk = jnp.concatenate([dk[:keys] + early_key, dk[keys:]], axis=0)
            dv = jnp.concatenate([dv[:keys] + early_value, dv[keys:]], axis=0)
            key_sum = dk if key_sum is None else key_sum + dk
            value_sum = dv if value_sum is None else value_sum + dv
        for total, column in ((key_sum, kv * HD), (value_sum, (KV + kv) * HD)):
            low = total.astype(jnp.bfloat16)
            for kind in range(3):
                block = low[kind * keys : (kind + 1) * keys].reshape(2 * slots, half, HD)
                if kind < 2:
                    dkv_ref[:, kind * half : (kind + 1) * half, column : column + HD] = block
                else:
                    dprev_ref[:, :, column : column + HD] = block


def attention(qpos, kpos, qg, kv, prev):
    slots, tok, _ = qg.shape
    return pl.pallas_call(
        attention_kernel,
        out_shape=(
            jax.ShapeDtypeStruct((slots, tok, KV * GROUP * HD), jnp.bfloat16),
            jax.ShapeDtypeStruct(kv.shape, jnp.bfloat16),
            jax.ShapeDtypeStruct(prev.shape, jnp.bfloat16),
        ),
        compiler_params=pltpu.CompilerParams(vmem_limit_bytes=48 * 1024 * 1024),
    )(qpos, kpos, qg, kv, prev)


def pack_kernel(first_ref, second_ref, out_ref, first_buf, second_buf, sems):
    pairs = ((first_ref, first_buf), (second_ref, second_buf))
    copies = [pltpu.make_async_copy(ref, buf, sems.at[i]) for i, (ref, buf) in enumerate(pairs)]
    for copy in copies:
        copy.start()
    wide = out_ref.shape[2] // 2
    for i, (_, buf) in enumerate(pairs):
        copies[i].wait()
        for block in range(out_ref.shape[0]):
            x = block % XN
            out_ref[block, :, i * wide : (i + 1) * wide] = buf[:, x * wide : (x + 1) * wide]


def pack(blocks, first, second):
    tok, total = first.shape
    return pl.pallas_call(
        pack_kernel,
        out_shape=jax.ShapeDtypeStruct((blocks, tok, 2 * total // XN), first.dtype),
        in_specs=[pl.BlockSpec(memory_space=pl.ANY)] * 2,
        scratch_shapes=[
            pltpu.VMEM(first.shape, first.dtype),
            pltpu.VMEM(second.shape, second.dtype),
            pltpu.SemaphoreType.DMA((2,)),
        ],
    )(first, second)


def add_kernel(dkv_ref, back_ref, out_ref):
    half = back_ref.shape[1]
    total = dkv_ref[:, :half].astype(jnp.float32) + back_ref[...].astype(jnp.float32)
    out_ref[:, :half] = total.astype(out_ref.dtype)
    out_ref[:, half:] = dkv_ref[:, half:]


def add_back(dkv, back):
    return pl.pallas_call(
        add_kernel,
        out_shape=jax.ShapeDtypeStruct(dkv.shape, dkv.dtype),
        compiler_params=pltpu.CompilerParams(vmem_limit_bytes=16 * 1024 * 1024),
    )(dkv, back)


def unpack_kernel(dq_ref, dkv_ref, query_ref, key_ref, value_ref):
    wide = dq_ref.shape[2]
    lines = KV * HD
    for x in range(XN):
        query_ref[:, x * wide : (x + 1) * wide] = dq_ref[x]
        for i, ref in enumerate((key_ref, value_ref)):
            source = slice(i * lines, (i + 1) * lines)
            total = dkv_ref[x, :, source].astype(jnp.float32)
            total = total + dkv_ref[XN + x, :, source].astype(jnp.float32)
            ref[:, x * lines : (x + 1) * lines] = total.astype(ref.dtype)


def unpack(dq, dkv):
    tok = dq.shape[1]
    shapes = [(tok, XN * dq.shape[2])] + [(tok, XN * KV * HD)] * 2
    return pl.pallas_call(
        unpack_kernel,
        out_shape=tuple(jax.ShapeDtypeStruct(shape, jnp.bfloat16) for shape in shapes),
        compiler_params=pltpu.CompilerParams(vmem_limit_bytes=16 * 1024 * 1024),
    )(dq, dkv)


def body(queries, keys, values, grad_out, order):
    groups = lax.axis_size("head")
    cycle = lax.axis_size("blk")
    mine = lax.axis_index("blk")
    tok = queries.shape[0]
    half = tok // 2
    slot_total = order.shape[0]
    teams = [list(range(t, t + XN)) for t in range(0, groups, XN)]
    ahead = [(i, (i + 1) % cycle) for i in range(cycle)]
    behind = [(j, i) for i, j in ahead]

    def team_exchange(array):
        return lax.all_to_all(array, "head", 0, 0, tiled=True, axis_index_groups=teams)

    def exchange(array):
        return lax.all_to_all(array, "head", 0, 0, tiled=True)

    kv = exchange(pack(groups, keys, values))
    prev = lax.ppermute(kv[:, :half], "blk", ahead)
    qg = pack(XN, queries, grad_out)
    qg, kv = lax.optimization_barrier((qg, kv))
    qg = team_exchange(qg)

    places = lax.dynamic_index_in_dim(order.reshape(groups, cycle), mine, axis=1, keepdims=False)
    offset = lax.iota(jnp.int32, half)
    early = (places[:, None] * half + offset[None, :]).reshape(groups * half)
    late = ((2 * slot_total - 1 - places)[:, None] * half + offset[None, :]).reshape(groups * half)
    kpos = jnp.stack([early, late], axis=1)
    team = lax.axis_index("head") // XN
    here = [lax.dynamic_slice_in_dim(p, team * XN * half, XN * half) for p in (early, late)]
    qpos = jnp.stack([jnp.tile(p, 2) for p in here], axis=0)

    dq, dkv, dprev = attention(qpos, kpos, qg, kv, prev)

    back = lax.ppermute(dprev, "blk", behind)
    dq = team_exchange(dq)
    dq, back = lax.optimization_barrier((dq, back))
    dkv = add_back(dkv, back)
    return unpack(dq, exchange(dkv))


def solution(mesh):
    rows = P(("head", "blk"), None)
    return jax.shard_map(
        body,
        mesh=mesh,
        in_specs=(rows, rows, rows, rows, P()),
        out_specs=(rows, rows, rows),
        check_vma=False,
    )
```

```python
import jax
import jax.numpy as jnp
from jax import lax
from jax.experimental import pallas as pl
from jax.experimental.pallas import tpu as pltpu
from jax.sharding import PartitionSpec as P

HD = 128
XN = 4
KV = 2
GROUP = 4
LOG2E = 1.4426950408889634
NEG = -1e30


def dot(left, right, left_dim, right_dim):
    return lax.dot_general(
        left, right, (((left_dim,), (right_dim,)), ((), ())), preferred_element_type=jnp.float32
    )


def attention_kernel(qpos_ref, kpos_ref, qg_ref, kv_ref, prev_ref, dq_ref, dkv_ref, dprev_ref):
    half = qg_ref.shape[1] // 2
    slots = qg_ref.shape[0]
    rows = slots * half
    scale = HD ** (-0.5)
    width = KV * GROUP * HD
    qpos = qpos_ref[...]
    kpos = kpos_ref[...]
    keys = kpos.shape[0]
    early_seen = kpos[:, 0:1] <= qpos[0:1, :]
    late_seen = kpos[:, 1:2] <= qpos[1:2, :]

    def columns(ref, start, stop, column):
        block = ref[:, start:stop, column : column + HD]
        return block.reshape(block.shape[0] * block.shape[1], HD)

    def tile(query, grad, key, value, seen, seen_from):
        logits = dot(key, query, 1, 1) * (scale * LOG2E)
        if seen_from == 0 and seen.shape[0] == key.shape[0]:
            logits = jnp.where(seen, logits, NEG)
        else:
            stop = seen_from + seen.shape[0]
            logits = jnp.concatenate(
                [
                    logits[:seen_from],
                    jnp.where(seen, logits[seen_from:stop], NEG),
                    logits[stop:],
                ],
                axis=0,
            )
        spread = dot(value, grad, 1, 1)
        top = jnp.max(logits, axis=0, keepdims=True)
        mass = jnp.exp2(logits - top)
        weights = mass * (1.0 / jnp.sum(mass, axis=0, keepdims=True))
        low = weights.astype(jnp.bfloat16)
        delta = jnp.sum(low.astype(jnp.float32) * spread, axis=0, keepdims=True)
        slopes = (weights * (spread - delta)).astype(jnp.bfloat16)
        return (
            dot(key, slopes, 0, 0).T * scale,
            dot(slopes, query, 1, 0) * scale,
            dot(low, grad, 1, 0),
        )

    for kv in range(KV):
        parts = []
        for column in (kv * HD, (KV + kv) * HD):
            parts.append(
                jnp.concatenate(
                    [
                        columns(kv_ref, 0, half, column),
                        columns(kv_ref, half, 2 * half, column),
                        columns(prev_ref, 0, half, column),
                    ],
                    axis=0,
                )
            )
        key, value = parts
        key_sum = None
        value_sum = None
        for pair in range(1):
            heads = [kv * GROUP + i for i in range(GROUP)]
            for kind in range(2):
                start, stop = kind * half, (kind + 1) * half
                query = jnp.concatenate(
                    [columns(qg_ref, start, stop, h * HD) for h in heads], axis=0
                )
                grad = jnp.concatenate(
                    [columns(qg_ref, start, stop, width + h * HD) for h in heads], axis=0
                )
                if kind == 0:
                    dq, dk, dv = tile(query, grad, key[:keys], value[:keys], early_seen, 0)
                    early_key, early_value = dk, dv
                else:
                    dq, dk, dv = tile(query, grad, key, value, late_seen, keys)
                for i, h in enumerate(heads):
                    dq_ref[:, start:stop, h * HD : (h + 1) * HD] = (
                        dq[i * rows : (i + 1) * rows].reshape(slots, half, HD).astype(jnp.bfloat16)
                    )
            dk = jnp.concatenate([dk[:keys] + early_key, dk[keys:]], axis=0)
            dv = jnp.concatenate([dv[:keys] + early_value, dv[keys:]], axis=0)
            key_sum = dk if key_sum is None else key_sum + dk
            value_sum = dv if value_sum is None else value_sum + dv
        for total, column in ((key_sum, kv * HD), (value_sum, (KV + kv) * HD)):
            low = total.astype(jnp.bfloat16)
            for kind in range(3):
                block = low[kind * keys : (kind + 1) * keys].reshape(2 * slots, half, HD)
                if kind < 2:
                    dkv_ref[:, kind * half : (kind + 1) * half, column : column + HD] = block
                else:
                    dprev_ref[:, :, column : column + HD] = block


def attention(qpos, kpos, qg, kv, prev):
    slots, tok, _ = qg.shape
    return pl.pallas_call(
        attention_kernel,
        out_shape=(
            jax.ShapeDtypeStruct((slots, tok, KV * GROUP * HD), jnp.bfloat16),
            jax.ShapeDtypeStruct(kv.shape, jnp.bfloat16),
            jax.ShapeDtypeStruct(prev.shape, jnp.bfloat16),
        ),
        compiler_params=pltpu.CompilerParams(vmem_limit_bytes=48 * 1024 * 1024),
    )(qpos, kpos, qg, kv, prev)


def pack_kernel(first_ref, second_ref, out_ref, first_buf, second_buf, sems):
    pairs = ((first_ref, first_buf), (second_ref, second_buf))
    copies = [pltpu.make_async_copy(ref, buf, sems.at[i]) for i, (ref, buf) in enumerate(pairs)]
    for copy in copies:
        copy.start()
    wide = out_ref.shape[2] // 2
    for i, (_, buf) in enumerate(pairs):
        copies[i].wait()
        for block in range(out_ref.shape[0]):
            x = block % XN
            out_ref[block, :, i * wide : (i + 1) * wide] = buf[:, x * wide : (x + 1) * wide]


def pack(blocks, first, second):
    tok, total = first.shape
    return pl.pallas_call(
        pack_kernel,
        out_shape=jax.ShapeDtypeStruct((blocks, tok, 2 * total // XN), first.dtype),
        in_specs=[pl.BlockSpec(memory_space=pl.ANY)] * 2,
        scratch_shapes=[
            pltpu.VMEM(first.shape, first.dtype),
            pltpu.VMEM(second.shape, second.dtype),
            pltpu.SemaphoreType.DMA((2,)),
        ],
    )(first, second)


def add_kernel(dkv_ref, back_ref, out_ref):
    half = back_ref.shape[1]
    total = dkv_ref[:, :half].astype(jnp.float32) + back_ref[...].astype(jnp.float32)
    out_ref[:, :half] = total.astype(out_ref.dtype)
    out_ref[:, half:] = dkv_ref[:, half:]


def add_back(dkv, back):
    return pl.pallas_call(
        add_kernel,
        out_shape=jax.ShapeDtypeStruct(dkv.shape, dkv.dtype),
        compiler_params=pltpu.CompilerParams(vmem_limit_bytes=16 * 1024 * 1024),
    )(dkv, back)


def unpack_kernel(dq_ref, dkv_ref, query_ref, key_ref, value_ref):
    wide = dq_ref.shape[2]
    lines = KV * HD
    for x in range(XN):
        query_ref[:, x * wide : (x + 1) * wide] = dq_ref[x]
        for i, ref in enumerate((key_ref, value_ref)):
            source = slice(i * lines, (i + 1) * lines)
            total = dkv_ref[x, :, source].astype(jnp.float32)
            total = total + dkv_ref[XN + x, :, source].astype(jnp.float32)
            ref[:, x * lines : (x + 1) * lines] = total.astype(ref.dtype)


def unpack(dq, dkv):
    tok = dq.shape[1]
    shapes = [(tok, XN * dq.shape[2])] + [(tok, XN * KV * HD)] * 2
    return pl.pallas_call(
        unpack_kernel,
        out_shape=tuple(jax.ShapeDtypeStruct(shape, jnp.bfloat16) for shape in shapes),
        compiler_params=pltpu.CompilerParams(vmem_limit_bytes=16 * 1024 * 1024),
    )(dq, dkv)


def body(queries, keys, values, grad_out, order):
    groups = lax.axis_size("head")
    cycle = lax.axis_size("blk")
    mine = lax.axis_index("blk")
    tok = queries.shape[0]
    half = tok // 2
    slot_total = order.shape[0]
    teams = [list(range(t, t + XN)) for t in range(0, groups, XN)]
    ahead = [(i, (i + 1) % cycle) for i in range(cycle)]
    behind = [(j, i) for i, j in ahead]

    def team_exchange(array):
        return lax.all_to_all(array, "head", 0, 0, tiled=True, axis_index_groups=teams)

    def exchange(array):
        return lax.all_to_all(array, "head", 0, 0, tiled=True)

    kv = exchange(pack(groups, keys, values))
    prev = lax.ppermute(kv[:, :half], "blk", ahead)
    qg = pack(XN, queries, grad_out)
    qg, kv = lax.optimization_barrier((qg, kv))
    qg = team_exchange(qg)

    places = lax.dynamic_index_in_dim(order.reshape(groups, cycle), mine, axis=1, keepdims=False)
    offset = lax.iota(jnp.int32, half)
    early = (places[:, None] * half + offset[None, :]).reshape(groups * half)
    late = ((2 * slot_total - 1 - places)[:, None] * half + offset[None, :]).reshape(groups * half)
    kpos = jnp.stack([early, late], axis=1)
    team = lax.axis_index("head") // XN
    here = [lax.dynamic_slice_in_dim(p, team * XN * half, XN * half) for p in (early, late)]
    qpos = jnp.stack([jnp.tile(p, GROUP) for p in here], axis=0)

    dq, dkv, dprev = attention(qpos, kpos, qg, kv, prev)

    back = lax.ppermute(dprev, "blk", behind)
    dq = team_exchange(dq)
    dq, back = lax.optimization_barrier((dq, back))
    dkv = add_back(dkv, back)
    return unpack(dq, exchange(dkv))


def solution(mesh):
    rows = P(("head", "blk"), None)
    return jax.shard_map(
        body,
        mesh=mesh,
        in_specs=(rows, rows, rows, rows, P()),
        out_specs=(rows, rows, rows),
        check_vma=False,
    )
```

```python
import jax
import jax.numpy as jnp
from jax import lax
from jax.experimental import pallas as pl
from jax.experimental.pallas import tpu as pltpu
from jax.sharding import PartitionSpec as P

HD = 128
XN = 4
KV = 2
GROUP = 4
LOG2E = 1.4426950408889634
NEG = -1e30


def dot(left, right, left_dim, right_dim):
    return lax.dot_general(
        left, right, (((left_dim,), (right_dim,)), ((), ())), preferred_element_type=jnp.float32
    )


def columns(ref, start, stop, column):
    block = ref[:, start:stop, column : column + HD]
    return block.reshape(block.shape[0] * block.shape[1], HD)


def tile(qg_ref, dq_ref, kv, kind, out_start, key, value, seen, seen_from):
    scale = HD ** (-0.5)
    half = qg_ref.shape[1] // 2
    slots = qg_ref.shape[0]
    rows = slots * half
    width = KV * GROUP * HD
    start, stop = kind * half, (kind + 1) * half
    heads = [kv * GROUP + i for i in range(GROUP)]
    query, grad = [
        jnp.concatenate([columns(qg_ref, start, stop, first + h * HD) for h in heads], axis=0)
        for first in (0, width)
    ]
    logits = dot(key, query, 1, 1) * (scale * LOG2E)
    seen_stop = seen_from + seen.shape[0]
    masked = jnp.where(seen, logits[seen_from:seen_stop], NEG)
    if seen.shape[0] == key.shape[0]:
        logits = masked
    else:
        logits = jnp.concatenate([logits[:seen_from], masked, logits[seen_stop:]], axis=0)
    spread = dot(value, grad, 1, 1)
    top = jnp.max(logits, axis=0, keepdims=True)
    mass = jnp.exp2(logits - top)
    weights = mass * (1.0 / jnp.sum(mass, axis=0, keepdims=True))
    low = weights.astype(jnp.bfloat16)
    delta = jnp.sum(low.astype(jnp.float32) * spread, axis=0, keepdims=True)
    slopes = (weights * (spread - delta)).astype(jnp.bfloat16)
    dq = dot(key, slopes, 0, 0).T * scale
    for i, h in enumerate(heads):
        dq_ref[:, out_start : out_start + half, h * HD : (h + 1) * HD] = (
            dq[i * rows : (i + 1) * rows].reshape(slots, half, HD).astype(jnp.bfloat16)
        )
    return dot(slopes, query, 1, 0) * scale, dot(low, grad, 1, 0)


def early_kernel(qpos_ref, kpos_ref, qg_ref, kv_ref, dq_ref, sum_ref):
    half = qg_ref.shape[1] // 2
    seen = kpos_ref[:, 0:1] <= qpos_ref[0:1, :]
    for kv in range(KV):
        key, value = [columns(kv_ref, 0, half, (i * KV + kv) * HD) for i in range(2)]
        for i, total in enumerate(tile(qg_ref, dq_ref, kv, 0, 0, key, value, seen, 0)):
            sum_ref[i * KV + kv] = total


def late_kernel(
    qpos_ref, kpos_ref, qg_ref, kv_ref, prev_ref, dqe_ref, sum_ref, dq_ref, dkv_ref, dprev_ref
):
    half = qg_ref.shape[1] // 2
    slots = kv_ref.shape[0]
    keys = kpos_ref.shape[0]
    seen = kpos_ref[:, 1:2] <= qpos_ref[1:2, :]
    dq_ref[:, :half, :] = dqe_ref[...]
    for kv in range(KV):
        key, value = [
            jnp.concatenate(
                [
                    columns(kv_ref, 0, half, column),
                    columns(kv_ref, half, 2 * half, column),
                    columns(prev_ref, 0, half, column),
                ],
                axis=0,
            )
            for column in (kv * HD, (KV + kv) * HD)
        ]
        for i, total in enumerate(tile(qg_ref, dq_ref, kv, 1, half, key, value, seen, keys)):
            column = (i * KV + kv) * HD
            pieces = [
                total[:keys] + sum_ref[i * KV + kv],
                total[keys : 2 * keys],
                total[2 * keys :],
            ]
            pieces = [p.astype(jnp.bfloat16).reshape(slots, half, HD) for p in pieces]
            dkv_ref[:, :half, column : column + HD] = pieces[0]
            dkv_ref[:, half:, column : column + HD] = pieces[1]
            dprev_ref[:, :, column : column + HD] = pieces[2]


def attention(qpos, kpos, qg, kv, prev):
    slots, tok, _ = qg.shape
    wide = KV * GROUP * HD
    dq_early, sums = pl.pallas_call(
        early_kernel,
        out_shape=(
            jax.ShapeDtypeStruct((slots, tok // 2, wide), jnp.bfloat16),
            jax.ShapeDtypeStruct((2 * KV, kpos.shape[0], HD), jnp.float32),
        ),
        compiler_params=pltpu.CompilerParams(vmem_limit_bytes=40 * 1024 * 1024),
    )(qpos, kpos, qg, kv)
    return pl.pallas_call(
        late_kernel,
        out_shape=(
            jax.ShapeDtypeStruct((slots, tok, wide), jnp.bfloat16),
            jax.ShapeDtypeStruct(kv.shape, jnp.bfloat16),
            jax.ShapeDtypeStruct(prev.shape, jnp.bfloat16),
        ),
        compiler_params=pltpu.CompilerParams(vmem_limit_bytes=48 * 1024 * 1024),
    )(qpos, kpos, qg, kv, prev, dq_early, sums)


def pack_kernel(first_ref, second_ref, out_ref, first_buf, second_buf, sems):
    pairs = ((first_ref, first_buf), (second_ref, second_buf))
    copies = [pltpu.make_async_copy(ref, buf, sems.at[i]) for i, (ref, buf) in enumerate(pairs)]
    for copy in copies:
        copy.start()
    wide = out_ref.shape[2] // 2
    for i, (_, buf) in enumerate(pairs):
        copies[i].wait()
        for block in range(out_ref.shape[0]):
            x = block % XN
            out_ref[block, :, i * wide : (i + 1) * wide] = buf[:, x * wide : (x + 1) * wide]


def pack(blocks, first, second):
    tok, total = first.shape
    return pl.pallas_call(
        pack_kernel,
        out_shape=jax.ShapeDtypeStruct((blocks, tok, 2 * total // XN), first.dtype),
        in_specs=[pl.BlockSpec(memory_space=pl.ANY)] * 2,
        scratch_shapes=[
            pltpu.VMEM(first.shape, first.dtype),
            pltpu.VMEM(second.shape, second.dtype),
            pltpu.SemaphoreType.DMA((2,)),
        ],
    )(first, second)


def add_kernel(dkv_ref, back_ref, out_ref):
    half = back_ref.shape[1]
    total = dkv_ref[:, :half].astype(jnp.float32) + back_ref[...].astype(jnp.float32)
    out_ref[:, :half] = total.astype(out_ref.dtype)
    out_ref[:, half:] = dkv_ref[:, half:]


def add_back(dkv, back):
    return pl.pallas_call(
        add_kernel,
        out_shape=jax.ShapeDtypeStruct(dkv.shape, dkv.dtype),
        compiler_params=pltpu.CompilerParams(vmem_limit_bytes=16 * 1024 * 1024),
    )(dkv, back)


def unpack_kernel(dq_ref, dkv_ref, query_ref, key_ref, value_ref):
    wide = dq_ref.shape[2]
    lines = KV * HD
    for x in range(XN):
        query_ref[:, x * wide : (x + 1) * wide] = dq_ref[x]
        for i, ref in enumerate((key_ref, value_ref)):
            source = slice(i * lines, (i + 1) * lines)
            total = dkv_ref[x, :, source].astype(jnp.float32)
            total = total + dkv_ref[XN + x, :, source].astype(jnp.float32)
            ref[:, x * lines : (x + 1) * lines] = total.astype(ref.dtype)


def unpack(dq, dkv):
    tok = dq.shape[1]
    shapes = [(tok, XN * dq.shape[2])] + [(tok, XN * KV * HD)] * 2
    return pl.pallas_call(
        unpack_kernel,
        out_shape=tuple(jax.ShapeDtypeStruct(shape, jnp.bfloat16) for shape in shapes),
        compiler_params=pltpu.CompilerParams(vmem_limit_bytes=16 * 1024 * 1024),
    )(dq, dkv)


def body(queries, keys, values, grad_out, order):
    groups = lax.axis_size("head")
    cycle = lax.axis_size("blk")
    mine = lax.axis_index("blk")
    tok = queries.shape[0]
    half = tok // 2
    slot_total = order.shape[0]
    teams = [list(range(t, t + XN)) for t in range(0, groups, XN)]
    ahead = [(i, (i + 1) % cycle) for i in range(cycle)]
    behind = [(j, i) for i, j in ahead]

    def team_exchange(array):
        return lax.all_to_all(array, "head", 0, 0, tiled=True, axis_index_groups=teams)

    def exchange(array):
        return lax.all_to_all(array, "head", 0, 0, tiled=True)

    kv = exchange(pack(groups, keys, values))
    prev = lax.ppermute(kv[:, :half], "blk", ahead)
    qg = pack(XN, queries, grad_out)
    qg, kv = lax.optimization_barrier((qg, kv))
    qg = team_exchange(qg)

    places = lax.dynamic_index_in_dim(order.reshape(groups, cycle), mine, axis=1, keepdims=False)
    offset = lax.iota(jnp.int32, half)
    early = (places[:, None] * half + offset[None, :]).reshape(groups * half)
    late = ((2 * slot_total - 1 - places)[:, None] * half + offset[None, :]).reshape(groups * half)
    kpos = jnp.stack([early, late], axis=1)
    team = lax.axis_index("head") // XN
    here = [lax.dynamic_slice_in_dim(p, team * XN * half, XN * half) for p in (early, late)]
    qpos = jnp.stack([jnp.tile(p, GROUP) for p in here], axis=0)

    dq, dkv, dprev = attention(qpos, kpos, qg, kv, prev)

    back = lax.ppermute(dprev, "blk", behind)
    dq = team_exchange(dq)
    dq, back = lax.optimization_barrier((dq, back))
    dkv = add_back(dkv, back)
    return unpack(dq, exchange(dkv))


def solution(mesh):
    rows = P(("head", "blk"), None)
    return jax.shard_map(
        body,
        mesh=mesh,
        in_specs=(rows, rows, rows, rows, P()),
        out_specs=(rows, rows, rows),
        check_vma=False,
    )
```

```python
import jax
import jax.numpy as jnp
from jax import lax
from jax.experimental import pallas as pl
from jax.experimental.pallas import tpu as pltpu
from jax.sharding import PartitionSpec as P

HD = 128
XN = 4
KV = 2
GROUP = 4
LOG2E = 1.4426950408889634
NEG = -1e30


def dot(left, right, left_dim, right_dim):
    return lax.dot_general(
        left, right, (((left_dim,), (right_dim,)), ((), ())), preferred_element_type=jnp.float32
    )


def columns(ref, start, stop, column):
    block = ref[:, start:stop, column : column + HD]
    return block.reshape(block.shape[0] * block.shape[1], HD)


def attention_kernel(qpos_ref, kpos_ref, qg_ref, full_ref, dq_ref, dkv_ref, dprev_ref):
    half = qg_ref.shape[1] // 2
    slots = qg_ref.shape[0]
    rows = slots * half
    scale = HD ** (-0.5)
    width = KV * GROUP * HD
    qpos = qpos_ref[...]
    kpos = kpos_ref[...].T
    keys = kpos.shape[0]
    early_seen = kpos[:, 0:1] <= qpos[0:1, :]
    late_seen = kpos[:, 1:2] <= qpos[1:2, :]

    def tile(query, grad, key, value, seen, seen_from):
        logits = dot(key, query, 1, 1) * (scale * LOG2E)
        if seen_from == 0 and seen.shape[0] == key.shape[0]:
            logits = jnp.where(seen, logits, NEG)
        else:
            stop = seen_from + seen.shape[0]
            logits = jnp.concatenate(
                [
                    logits[:seen_from],
                    jnp.where(seen, logits[seen_from:stop], NEG),
                    logits[stop:],
                ],
                axis=0,
            )
        spread = dot(value, grad, 1, 1)
        top = jnp.max(logits, axis=0, keepdims=True)
        mass = jnp.exp2(logits - top)
        weights = mass * (1.0 / jnp.sum(mass, axis=0, keepdims=True))
        low = weights.astype(jnp.bfloat16)
        delta = jnp.sum(low.astype(jnp.float32) * spread, axis=0, keepdims=True)
        slopes = (weights * (spread - delta)).astype(jnp.bfloat16)
        return (
            dot(key, slopes, 0, 0).T * scale,
            dot(slopes, query, 1, 0) * scale,
            dot(low, grad, 1, 0),
        )

    for kv in range(KV):
        key, value = full_ref[kv], full_ref[KV + kv]
        key_sum = None
        value_sum = None
        for pair in range(1):
            heads = [kv * GROUP + i for i in range(GROUP)]
            for kind in range(2):
                start, stop = kind * half, (kind + 1) * half
                query = jnp.concatenate(
                    [columns(qg_ref, start, stop, h * HD) for h in heads], axis=0
                )
                grad = jnp.concatenate(
                    [columns(qg_ref, start, stop, width + h * HD) for h in heads], axis=0
                )
                if kind == 0:
                    dq, dk, dv = tile(query, grad, key[:keys], value[:keys], early_seen, 0)
                    early_key, early_value = dk, dv
                else:
                    dq, dk, dv = tile(query, grad, key, value, late_seen, keys)
                for i, h in enumerate(heads):
                    dq_ref[:, start:stop, h * HD : (h + 1) * HD] = (
                        dq[i * rows : (i + 1) * rows].reshape(slots, half, HD).astype(jnp.bfloat16)
                    )
            dk = jnp.concatenate([dk[:keys] + early_key, dk[keys:]], axis=0)
            dv = jnp.concatenate([dv[:keys] + early_value, dv[keys:]], axis=0)
            key_sum = dk if key_sum is None else key_sum + dk
            value_sum = dv if value_sum is None else value_sum + dv
        for total, column in ((key_sum, kv * HD), (value_sum, (KV + kv) * HD)):
            low = total.astype(jnp.bfloat16)
            for kind in range(3):
                block = low[kind * keys : (kind + 1) * keys].reshape(2 * slots, half, HD)
                if kind < 2:
                    dkv_ref[:, kind * half : (kind + 1) * half, column : column + HD] = block
                else:
                    dprev_ref[:, :, column : column + HD] = block


def join_kernel(kv_ref, prev_ref, full_ref):
    half = prev_ref.shape[1]
    rows = prev_ref.shape[0] * half
    for i in range(2 * KV):
        full_ref[i, :rows] = columns(kv_ref, 0, half, i * HD)
        full_ref[i, rows : 2 * rows] = columns(kv_ref, half, 2 * half, i * HD)
        full_ref[i, 2 * rows :] = columns(prev_ref, 0, half, i * HD)


def join(kv, prev):
    rows = prev.shape[0] * prev.shape[1]
    return pl.pallas_call(
        join_kernel,
        out_shape=jax.ShapeDtypeStruct((2 * KV, 3 * rows, HD), kv.dtype),
        compiler_params=pltpu.CompilerParams(vmem_limit_bytes=16 * 1024 * 1024),
    )(kv, prev)


def attention(qpos, kpos, qg, full):
    slots, tok, _ = qg.shape
    lines = 2 * KV * HD
    return pl.pallas_call(
        attention_kernel,
        out_shape=(
            jax.ShapeDtypeStruct((slots, tok, KV * GROUP * HD), jnp.bfloat16),
            jax.ShapeDtypeStruct((2 * slots, tok, lines), jnp.bfloat16),
            jax.ShapeDtypeStruct((2 * slots, tok // 2, lines), jnp.bfloat16),
        ),
        compiler_params=pltpu.CompilerParams(vmem_limit_bytes=48 * 1024 * 1024),
    )(qpos, kpos, qg, full)


def pack_kernel(first_ref, second_ref, out_ref, first_buf, second_buf, sems):
    pairs = ((first_ref, first_buf), (second_ref, second_buf))
    copies = [pltpu.make_async_copy(ref, buf, sems.at[i]) for i, (ref, buf) in enumerate(pairs)]
    for copy in copies:
        copy.start()
    wide = out_ref.shape[2] // 2
    for i, (_, buf) in enumerate(pairs):
        copies[i].wait()
        for block in range(out_ref.shape[0]):
            x = block % XN
            out_ref[block, :, i * wide : (i + 1) * wide] = buf[:, x * wide : (x + 1) * wide]


def pack(blocks, first, second):
    tok, total = first.shape
    return pl.pallas_call(
        pack_kernel,
        out_shape=jax.ShapeDtypeStruct((blocks, tok, 2 * total // XN), first.dtype),
        in_specs=[pl.BlockSpec(memory_space=pl.ANY)] * 2,
        scratch_shapes=[
            pltpu.VMEM(first.shape, first.dtype),
            pltpu.VMEM(second.shape, second.dtype),
            pltpu.SemaphoreType.DMA((2,)),
        ],
    )(first, second)


def add_kernel(dkv_ref, back_ref, out_ref):
    half = back_ref.shape[1]
    total = dkv_ref[:, :half].astype(jnp.float32) + back_ref[...].astype(jnp.float32)
    out_ref[:, :half] = total.astype(out_ref.dtype)
    out_ref[:, half:] = dkv_ref[:, half:]


def add_back(dkv, back):
    return pl.pallas_call(
        add_kernel,
        out_shape=jax.ShapeDtypeStruct(dkv.shape, dkv.dtype),
        compiler_params=pltpu.CompilerParams(vmem_limit_bytes=16 * 1024 * 1024),
    )(dkv, back)


def unpack_kernel(dq_ref, dkv_ref, query_ref, key_ref, value_ref):
    wide = dq_ref.shape[2]
    lines = KV * HD
    for x in range(XN):
        query_ref[:, x * wide : (x + 1) * wide] = dq_ref[x]
        for i, ref in enumerate((key_ref, value_ref)):
            source = slice(i * lines, (i + 1) * lines)
            total = dkv_ref[x, :, source].astype(jnp.float32)
            total = total + dkv_ref[XN + x, :, source].astype(jnp.float32)
            ref[:, x * lines : (x + 1) * lines] = total.astype(ref.dtype)


def unpack(dq, dkv):
    tok = dq.shape[1]
    shapes = [(tok, XN * dq.shape[2])] + [(tok, XN * KV * HD)] * 2
    return pl.pallas_call(
        unpack_kernel,
        out_shape=tuple(jax.ShapeDtypeStruct(shape, jnp.bfloat16) for shape in shapes),
        compiler_params=pltpu.CompilerParams(vmem_limit_bytes=16 * 1024 * 1024),
    )(dq, dkv)


def body(queries, keys, values, grad_out, order):
    groups = lax.axis_size("head")
    cycle = lax.axis_size("blk")
    mine = lax.axis_index("blk")
    tok = queries.shape[0]
    half = tok // 2
    slot_total = order.shape[0]
    teams = [list(range(t, t + XN)) for t in range(0, groups, XN)]
    ahead = [(i, (i + 1) % cycle) for i in range(cycle)]
    behind = [(j, i) for i, j in ahead]

    def team_exchange(array):
        return lax.all_to_all(array, "head", 0, 0, tiled=True, axis_index_groups=teams)

    def exchange(array):
        return lax.all_to_all(array, "head", 0, 0, tiled=True)

    places = lax.dynamic_index_in_dim(order.reshape(groups, cycle), mine, axis=1, keepdims=False)
    offset = lax.iota(jnp.int32, half)
    early = (places[:, None] * half + offset[None, :]).reshape(groups * half)
    late = ((2 * slot_total - 1 - places)[:, None] * half + offset[None, :]).reshape(groups * half)
    kpos = jnp.stack([early, late] * 4, axis=0).astype(jnp.float32)
    team = lax.axis_index("head") // XN
    here = [lax.dynamic_slice_in_dim(p, team * XN * half, XN * half) for p in (early, late)]
    qpos = jnp.stack([jnp.tile(p, GROUP) for p in here], axis=0).astype(jnp.float32)

    kv = exchange(pack(groups, keys, values))
    qg = pack(XN, queries, grad_out)
    kv, qpos, kpos = lax.optimization_barrier((kv, qpos, kpos))
    qg, sent = lax.optimization_barrier((qg, kv[:, :half]))
    prev = lax.ppermute(sent, "blk", ahead)
    qg = team_exchange(qg)

    dq, dkv, dprev = attention(qpos, kpos, qg, join(kv, prev))

    back = lax.ppermute(dprev, "blk", behind)
    dq = team_exchange(dq)
    dq, back = lax.optimization_barrier((dq, back))
    dkv = add_back(dkv, back)
    return unpack(dq, exchange(dkv))


def solution(mesh):
    rows = P(("head", "blk"), None)
    return jax.shard_map(
        body,
        mesh=mesh,
        in_specs=(rows, rows, rows, rows, P()),
        out_specs=(rows, rows, rows),
        check_vma=False,
    )
```

```python
import jax
import jax.numpy as jnp
from jax import lax
from jax.experimental import pallas as pl
from jax.experimental.pallas import tpu as pltpu
from jax.sharding import PartitionSpec as P

HD = 128
XN = 4
KV = 2
GROUP = 4
LOG2E = 1.4426950408889634
NEG = -1e30


def dot(left, right, left_dim, right_dim):
    return lax.dot_general(
        left, right, (((left_dim,), (right_dim,)), ((), ())), preferred_element_type=jnp.float32
    )


def columns(ref, start, stop, column):
    block = ref[:, start:stop, column : column + HD]
    return block.reshape(block.shape[0] * block.shape[1], HD)


def tile(qg_ref, dq_ref, kv, kind, out_start, key, value, seen, seen_from):
    scale = HD ** (-0.5)
    half = qg_ref.shape[1] // 2
    slots = qg_ref.shape[0]
    rows = slots * half
    width = KV * GROUP * HD
    start, stop = kind * half, (kind + 1) * half
    heads = [kv * GROUP + i for i in range(GROUP)]
    query, grad = [
        jnp.concatenate([columns(qg_ref, start, stop, first + h * HD) for h in heads], axis=0)
        for first in (0, width)
    ]
    logits = dot(key, query, 1, 1) * (scale * LOG2E)
    seen_stop = seen_from + seen.shape[0]
    masked = jnp.where(seen, logits[seen_from:seen_stop], NEG)
    if seen.shape[0] == key.shape[0]:
        logits = masked
    else:
        logits = jnp.concatenate([logits[:seen_from], masked, logits[seen_stop:]], axis=0)
    spread = dot(value, grad, 1, 1)
    top = jnp.max(logits, axis=0, keepdims=True)
    mass = jnp.exp2(logits - top)
    weights = mass * (1.0 / jnp.sum(mass, axis=0, keepdims=True))
    low = weights.astype(jnp.bfloat16)
    delta = jnp.sum(low.astype(jnp.float32) * spread, axis=0, keepdims=True)
    slopes = (weights * (spread - delta)).astype(jnp.bfloat16)
    dq = dot(key, slopes, 0, 0).T * scale
    for i, h in enumerate(heads):
        dq_ref[:, out_start : out_start + half, h * HD : (h + 1) * HD] = (
            dq[i * rows : (i + 1) * rows].reshape(slots, half, HD).astype(jnp.bfloat16)
        )
    return dot(slopes, query, 1, 0) * scale, dot(low, grad, 1, 0)


def early_kernel(qpos_ref, kpos_ref, qg_ref, kv_ref, dq_ref, sum_ref):
    half = qg_ref.shape[1] // 2
    seen = kpos_ref[...].T[:, 0:1] <= qpos_ref[0:1, :]
    for kv in range(KV):
        key, value = [columns(kv_ref, 0, half, (i * KV + kv) * HD) for i in range(2)]
        for i, total in enumerate(tile(qg_ref, dq_ref, kv, 0, 0, key, value, seen, 0)):
            sum_ref[i * KV + kv] = total


def late_kernel(
    qpos_ref, kpos_ref, qg_ref, kv_ref, prev_ref, dqe_ref, sum_ref, dq_ref, dkv_ref, dprev_ref
):
    half = qg_ref.shape[1] // 2
    slots = kv_ref.shape[0]
    keys = kpos_ref.shape[1]
    seen = kpos_ref[...].T[:, 1:2] <= qpos_ref[1:2, :]
    dq_ref[:, :half, :] = dqe_ref[...]
    for kv in range(KV):
        key, value = [
            jnp.concatenate(
                [
                    columns(kv_ref, 0, half, column),
                    columns(kv_ref, half, 2 * half, column),
                    columns(prev_ref, 0, half, column),
                ],
                axis=0,
            )
            for column in (kv * HD, (KV + kv) * HD)
        ]
        for i, total in enumerate(tile(qg_ref, dq_ref, kv, 1, half, key, value, seen, keys)):
            column = (i * KV + kv) * HD
            pieces = [
                total[:keys] + sum_ref[i * KV + kv],
                total[keys : 2 * keys],
                total[2 * keys :],
            ]
            pieces = [p.astype(jnp.bfloat16).reshape(slots, half, HD) for p in pieces]
            dkv_ref[:, :half, column : column + HD] = pieces[0]
            dkv_ref[:, half:, column : column + HD] = pieces[1]
            dprev_ref[:, :, column : column + HD] = pieces[2]


def attention(qpos, kpos, qg, kv, prev):
    slots, tok, _ = qg.shape
    wide = KV * GROUP * HD
    dq_early, sums = pl.pallas_call(
        early_kernel,
        out_shape=(
            jax.ShapeDtypeStruct((slots, tok // 2, wide), jnp.bfloat16),
            jax.ShapeDtypeStruct((2 * KV, kpos.shape[1], HD), jnp.float32),
        ),
        compiler_params=pltpu.CompilerParams(vmem_limit_bytes=40 * 1024 * 1024),
    )(qpos, kpos, qg, kv)
    return pl.pallas_call(
        late_kernel,
        out_shape=(
            jax.ShapeDtypeStruct((slots, tok, wide), jnp.bfloat16),
            jax.ShapeDtypeStruct(kv.shape, jnp.bfloat16),
            jax.ShapeDtypeStruct(prev.shape, jnp.bfloat16),
        ),
        compiler_params=pltpu.CompilerParams(vmem_limit_bytes=48 * 1024 * 1024),
    )(qpos, kpos, qg, kv, prev, dq_early, sums)


def pack_kernel(first_ref, second_ref, out_ref, first_buf, second_buf, sems):
    pairs = ((first_ref, first_buf), (second_ref, second_buf))
    copies = [pltpu.make_async_copy(ref, buf, sems.at[i]) for i, (ref, buf) in enumerate(pairs)]
    for copy in copies:
        copy.start()
    wide = out_ref.shape[2] // 2
    for i, (_, buf) in enumerate(pairs):
        copies[i].wait()
        for block in range(out_ref.shape[0]):
            x = block % XN
            out_ref[block, :, i * wide : (i + 1) * wide] = buf[:, x * wide : (x + 1) * wide]


def pack(blocks, first, second):
    tok, total = first.shape
    return pl.pallas_call(
        pack_kernel,
        out_shape=jax.ShapeDtypeStruct((blocks, tok, 2 * total // XN), first.dtype),
        in_specs=[pl.BlockSpec(memory_space=pl.ANY)] * 2,
        scratch_shapes=[
            pltpu.VMEM(first.shape, first.dtype),
            pltpu.VMEM(second.shape, second.dtype),
            pltpu.SemaphoreType.DMA((2,)),
        ],
    )(first, second)


def add_kernel(dkv_ref, back_ref, out_ref):
    half = back_ref.shape[1]
    total = dkv_ref[:, :half].astype(jnp.float32) + back_ref[...].astype(jnp.float32)
    out_ref[:, :half] = total.astype(out_ref.dtype)
    out_ref[:, half:] = dkv_ref[:, half:]


def add_back(dkv, back):
    return pl.pallas_call(
        add_kernel,
        out_shape=jax.ShapeDtypeStruct(dkv.shape, dkv.dtype),
        compiler_params=pltpu.CompilerParams(vmem_limit_bytes=16 * 1024 * 1024),
    )(dkv, back)


def unpack_kernel(dq_ref, dkv_ref, query_ref, key_ref, value_ref):
    wide = dq_ref.shape[2]
    lines = KV * HD
    for x in range(XN):
        query_ref[:, x * wide : (x + 1) * wide] = dq_ref[x]
        for i, ref in enumerate((key_ref, value_ref)):
            source = slice(i * lines, (i + 1) * lines)
            total = dkv_ref[x, :, source].astype(jnp.float32)
            total = total + dkv_ref[XN + x, :, source].astype(jnp.float32)
            ref[:, x * lines : (x + 1) * lines] = total.astype(ref.dtype)


def unpack(dq, dkv):
    tok = dq.shape[1]
    shapes = [(tok, XN * dq.shape[2])] + [(tok, XN * KV * HD)] * 2
    return pl.pallas_call(
        unpack_kernel,
        out_shape=tuple(jax.ShapeDtypeStruct(shape, jnp.bfloat16) for shape in shapes),
        compiler_params=pltpu.CompilerParams(vmem_limit_bytes=16 * 1024 * 1024),
    )(dq, dkv)


def body(queries, keys, values, grad_out, order):
    groups = lax.axis_size("head")
    cycle = lax.axis_size("blk")
    mine = lax.axis_index("blk")
    tok = queries.shape[0]
    half = tok // 2
    slot_total = order.shape[0]
    teams = [list(range(t, t + XN)) for t in range(0, groups, XN)]
    ahead = [(i, (i + 1) % cycle) for i in range(cycle)]
    behind = [(j, i) for i, j in ahead]

    def team_exchange(array):
        return lax.all_to_all(array, "head", 0, 0, tiled=True, axis_index_groups=teams)

    def exchange(array):
        return lax.all_to_all(array, "head", 0, 0, tiled=True)

    places = lax.dynamic_index_in_dim(order.reshape(groups, cycle), mine, axis=1, keepdims=False)
    offset = lax.iota(jnp.int32, half)
    early = (places[:, None] * half + offset[None, :]).reshape(groups * half)
    late = ((2 * slot_total - 1 - places)[:, None] * half + offset[None, :]).reshape(groups * half)
    kpos = jnp.stack([early, late] * 4, axis=0).astype(jnp.float32)
    team = lax.axis_index("head") // XN
    here = [lax.dynamic_slice_in_dim(p, team * XN * half, XN * half) for p in (early, late)]
    qpos = jnp.stack([jnp.tile(p, GROUP) for p in here], axis=0).astype(jnp.float32)

    kv = exchange(pack(groups, keys, values))
    qg = pack(XN, queries, grad_out)
    kv, qpos, kpos = lax.optimization_barrier((kv, qpos, kpos))
    qg, sent = lax.optimization_barrier((qg, kv[:, :half]))
    prev = lax.ppermute(sent, "blk", ahead)
    qg = team_exchange(qg)

    dq, dkv, dprev = attention(qpos, kpos, qg, kv, prev)

    back = lax.ppermute(dprev, "blk", behind)
    dq = team_exchange(dq)
    dq, back = lax.optimization_barrier((dq, back))
    dkv = add_back(dkv, back)
    return unpack(dq, exchange(dkv))


def solution(mesh):
    rows = P(("head", "blk"), None)
    return jax.shard_map(
        body,
        mesh=mesh,
        in_specs=(rows, rows, rows, rows, P()),
        out_specs=(rows, rows, rows),
        check_vma=False,
    )
```
